256 devices in a mesh: rep: 2 (over core), mp: 128 (over y, x, z).
Axes of the slice: x: 4, y: 4, z: 8, core: 2. Of those that a mesh axis runs over, the one named last changes fastest.
Arguments:
- lookup_block: int32 [2, 16384, 128, 4], P(None, ('rep', 'mp')), may hold values from 0 to 9
- lookup_offset: int32 [2, 16384, 128, 4], P(None, ('rep', 'mp')), may hold values from 0 to 63
- interaction_grad: bfloat16 [2, 16384, 128, 128], P(None, ('rep', 'mp')), may hold values from -1.25 to 1.25
- table: bfloat16 [393216, 256], P('mp'), may hold values from -0.3125 to 0.3125
- adagrad_state: float32 [393216], P('mp'), may hold values from 0.05 to 2
- touched_blocks: int32 [128, 10], P('mp'), may hold values from 0 to 47, as said below
- dither: int32 [128, 640, 256], P('mp'), may hold values from 0 to 32767
Outputs:
- new_table: bfloat16 [393216, 256], P('mp')
- new_state: float32 [393216], P('mp')
The draws below stay inside these ranges and needn't reach their ends.
Inputs may be any that keep to these rules, and one draw needn't show every extreme that they name: `touched_blocks`: each row names 10 different row blocks.
All inputs are finite; a program needn't handle non-finite values.
Results may differ from the reference program's by a relative error of at most 0.00055.
The reference program's roundings to bfloat16 on the way count: a program that leaves them out, or rounds other values in their place, can miss the bound.
Values may be sent and summed in bfloat16 or wider, within the bound.
No kernel may reach another device: no remote copies, remote signals or barrier semaphores. Data moves between devices by JAX's collectives and lax.ppermute only.
A program may use at most 128 MiB of HBM per device.

```python
import math
import jax
import jax.numpy as jnp
import numpy as np
from jax import lax

E = 256
MICRO = 2
BAG = 4
BLOCK = 64
TOUCH = 10
NBLK = 48
FEATURES = 128
SAMPLES = 16384
ROWS = 393216
N_MP = 128


def draw_touched_blocks(key, part):
    feature_keys = jax.random.split(jax.random.fold_in(key, 17), N_MP)

    def one_table(table_key):
        return jax.random.permutation(table_key, NBLK)[:TOUCH]
    return jax.vmap(one_table)(feature_keys).astype(jnp.int32)


def set_ends(values, stream_key, least, largest):
    extent = values.shape
    index_at = [jax.random.randint(jax.random.fold_in(stream_key, axis), (), 0, extent[axis]) for axis in range(len(extent))]
    values = values.at[tuple(index_at)].set(least)
    longest = extent.index(max(extent))
    index_at[longest] = (index_at[longest] + 1) % extent[longest]
    return values.at[tuple(index_at)].set(largest)


def block_scale(stream_key, shape, cuts, least, largest):
    level = 1.0
    for axis_at, parts in cuts:
        heights = jax.random.uniform(jax.random.fold_in(jax.random.fold_in(stream_key, 6), axis_at), (parts,), jnp.float32, least / len(cuts), largest / len(cuts))
        level = level * jnp.repeat(jnp.exp(heights), shape[axis_at] // parts).reshape((-1,) + (1,) * (len(shape) - 1 - axis_at))
    return level


def rank_table(number_of, skew):
    loads = [(1 << 20) // math.isqrt(grade ** skew) + 1 for grade in range(1, number_of + 1)]
    scale = 1 + sum(loads) // (1 << 30)
    return np.cumsum(np.array([max(1, weight // scale) for weight in loads]))


def ranked(key, shape, number_of, skew):
    grid = rank_table(number_of, skew)
    lot = jax.random.randint(jax.random.fold_in(key, 1), shape, 0, int(grid[number_of - 1]))
    grade = jnp.searchsorted(jnp.asarray(grid, jnp.int32), lot, side="right")
    return jax.random.permutation(jax.random.fold_in(key, 2), number_of)[grade].astype(jnp.int32)


def scatter_about(own_key, dims, scale, most, shards=(), held_as=jnp.bfloat16):
    loudness = block_scale(own_key, dims, shards, -0.22, 0.18) if shards else 1.0
    array = jax.random.normal(own_key, dims, jnp.float32) * scale * loudness
    return jnp.minimum(jnp.maximum(array, -most), most).astype(held_as)


def setup_inputs(seed: int = 0) -> dict:
    splits = jax.random.split(jax.random.key(seed), 8)
    return {
        "lookup_block": set_ends(ranked(splits[0], (MICRO, SAMPLES, FEATURES, BAG), TOUCH, 1), jax.random.fold_in(splits[0], 3), 0, TOUCH - 1).astype(jnp.int32),
        "lookup_offset": set_ends(jax.random.randint(splits[1], (MICRO, SAMPLES, FEATURES, BAG), 0, BLOCK), jax.random.fold_in(splits[1], 1), 0, BLOCK - 1).astype(jnp.int32),
        "interaction_grad": scatter_about(splits[2], (MICRO, SAMPLES, FEATURES, FEATURES), (FEATURES ** -0.5), 1.25, ((1, 256),)),
        "table": scatter_about(splits[3], (ROWS, E), 0.02, 0.3125, ((0, 128),)),
        "adagrad_state": jnp.clip(jnp.exp(math.log(2.0) - 3.6888794 * jax.random.uniform(splits[4], (ROWS,), jnp.float32) ** block_scale(splits[4], (ROWS,), ((0, 128),), -0.2, 0.2)), 0.05, 2.0),
        "touched_blocks": draw_touched_blocks(jax.random.fold_in(splits[7], 71), 0),
        "dither": set_ends(jax.random.randint(splits[6], (FEATURES, TOUCH * BLOCK, E), 0, 32768), jax.random.fold_in(splits[6], 1), 0, 32767).astype(jnp.int32),
    }


LEARN_RATE = 0.1
POOL_DECAY = 0.5
DITHER_UNIT = 2.0 ** (-15)
SMALLEST = 2.0 ** (-14)

def dither_round(weights, dither_bits):
    magnitude = jnp.maximum(jnp.abs(weights), SMALLEST)
    spacing = jnp.exp2(jnp.floor(jnp.log2(magnitude)) - 7.0)
    grid_level = jnp.floor(weights / spacing + dither_bits.astype(jnp.float32) * DITHER_UNIT)
    return (grid_level * spacing).astype(jnp.bfloat16)

def pairwise(pooled_rows, cotangent):
    pooled_wide = pooled_rows.astype(jnp.float32)
    cot_wide = cotangent.astype(jnp.float32)
    forward = jnp.einsum('bfg,bge->bfe', cot_wide, pooled_wide)
    backward = jnp.einsum('bgf,bge->bfe', cot_wide, pooled_wide)
    return (forward + backward + POOL_DECAY * pooled_wide).astype(jnp.bfloat16)

def reference(lookup_block, lookup_offset, interaction_grad, table, adagrad_state, touched_blocks, dither):
    slab_size = TOUCH * BLOCK
    table_blocks = table.reshape(N_MP, NBLK, BLOCK, E)
    feature_ids = jnp.arange(N_MP, dtype=jnp.int32)[:, None]
    chosen = table_blocks[feature_ids, touched_blocks]
    slab_table = chosen.reshape(N_MP * slab_size, E)
    feature_base = (jnp.arange(N_MP, dtype=jnp.int32) * slab_size)[None, None, :, None]
    slab_index = (lookup_block * BLOCK + lookup_offset + feature_base).astype(jnp.int32)
    sample_block = math.gcd(256, SAMPLES)
    steps_count = MICRO * SAMPLES // sample_block
    blocked_index = slab_index.reshape(steps_count, sample_block, N_MP, BAG)
    blocked_cot = interaction_grad.reshape(steps_count, sample_block, N_MP, N_MP)

    def accumulate(carry, pieces):
        index_piece, cot_piece = pieces
        gathered = slab_table[index_piece].astype(jnp.float32)
        pooled_rows = lax.optimization_barrier(jnp.sum(gathered, axis=2)).astype(jnp.bfloat16)
        back_rows = pairwise(pooled_rows, cot_piece).astype(jnp.float32)
        spread = jnp.broadcast_to(back_rows[:, :, None, :], gathered.shape).reshape(-1, E)
        carry = carry + jax.ops.segment_sum(spread, index_piece.reshape(-1), num_segments=N_MP * slab_size)
        return (carry, None)
    start_grad = jnp.zeros((N_MP * slab_size, E), jnp.float32)
    slab_grad, _ = lax.scan(accumulate, start_grad, (blocked_index, blocked_cot))
    state_blocks = adagrad_state.reshape(N_MP, NBLK, BLOCK)
    state_slab = state_blocks[feature_ids, touched_blocks].reshape(N_MP * slab_size)
    state_next = state_slab + lax.optimization_barrier(jnp.mean(slab_grad * slab_grad, axis=-1))
    moved = slab_table.astype(jnp.float32) - LEARN_RATE * slab_grad / (jnp.sqrt(state_next) + 1e-08)[:, None]
    rounded = dither_round(moved, dither.reshape(N_MP * slab_size, E))
    new_table = table_blocks.at[feature_ids, touched_blocks].set(rounded.reshape(N_MP, TOUCH, BLOCK, E))
    new_state = state_blocks.at[feature_ids, touched_blocks].set(state_next.reshape(N_MP, TOUCH, BLOCK))
    return (new_table.reshape(ROWS, E), new_state.reshape(ROWS))
```

```python
import jax
import jax.numpy as jnp
from jax import lax
from jax.experimental import pallas as pl
from jax.experimental.pallas import tpu as pltpu
from jax.sharding import Mesh
from jax.sharding import PartitionSpec as P

BLOCK = 64
LEARN_RATE = 0.1
POOL_DECAY = 0.5
DITHER_UNIT = 2.0 ** (-15)
SMALLEST = 2.0 ** (-14)

NY, NX, NZ = 4, 4, 8
LINE = 4
HALF = 128
SLAB = 640
BAG = 4
AXES = ("rep", "y", "x", "z")


def device_id(r, y, x, z):
    return ((r * NY + y) * NX + x) * NZ + z


def line_groups():
    first = [[device_id(0, y, x, z) for x in range(NX)] for y in range(NY) for z in range(NZ)]
    second = [[device_id(1, y, x, z) for y in range(NY)] for x in range(NX) for z in range(NZ)]
    return first + second


def ring_pairs(step):
    pairs = []
    for y in range(NY):
        for x in range(NX):
            for z in range(NZ):
                pairs.append((device_id(0, y, x, z), device_id(0, (y + step) % NY, x, z)))
                pairs.append((device_id(1, y, x, z), device_id(1, y, (x + step) % NX, z)))
    return pairs


def ring_send(value, step):
    return lax.ppermute(value, AXES, ring_pairs(step))


def line_exchange(value):
    return lax.all_to_all(value, AXES, 0, 0, tiled=True, axis_index_groups=line_groups())


def swap_cores(value):
    return lax.ppermute(value, "rep", [(0, 1), (1, 0)])


def counts_of(columns, iota):
    one = jnp.ones((), jnp.bfloat16)
    zero = jnp.zeros((), jnp.bfloat16)
    total = None
    for column in columns:
        hit = jnp.where(column == iota, one, zero)
        total = hit if total is None else total + hit
    return total


def pool_kernel(k, chips, samples, idx_ref, slab_ref, *rest):
    out_ref, buffer = rest[-2:]
    rows = chips * samples
    idx = idx_ref[...].reshape(rows, 128)
    iota = lax.broadcasted_iota(jnp.int16, (rows, SLAB), 1)
    for z in range(NZ):
        base = k * 32 + z * BAG
        hits = counts_of([idx[:, base + j : base + j + 1] for j in range(BAG)], iota)
        rows_sum = jnp.dot(hits, slab_ref[z], preferred_element_type=jnp.float32)
        buffer[pl.ds(z, rows, stride=NZ), :] = rows_sum
    out_ref[...] = buffer[...].astype(jnp.bfloat16).reshape(chips, samples, 1, NZ, HALF)


def pool_rows(k, idx, slabs, previous):
    samples = idx.shape[1]
    chips = 2
    operands = [idx, slabs]
    in_specs = [
        pl.BlockSpec((chips, samples, 128), lambda i: (i, 0, 0)),
        pl.BlockSpec((NZ, SLAB, HALF), lambda i: (0, 0, 0)),
    ]
    aliases = {}
    if previous is not None:
        operands.append(previous)
        in_specs.append(pl.BlockSpec(memory_space=pl.ANY))
        aliases = {2: 0}
    return pl.pallas_call(
        lambda *refs: pool_kernel(k, chips, samples, *refs),
        out_shape=jax.ShapeDtypeStruct((LINE, samples, 4, NZ, HALF), jnp.bfloat16),
        grid=(LINE // chips,),
        in_specs=in_specs,
        out_specs=pl.BlockSpec((chips, samples, 1, NZ, HALF), lambda i: (i, 0, k, 0, 0)),
        scratch_shapes=[pltpu.VMEM((chips * samples * NZ, HALF), jnp.float32)],
        input_output_aliases=aliases,
        compiler_params=pltpu.CompilerParams(vmem_limit_bytes=48 << 20),
        cost_estimate=pl.CostEstimate(
            flops=2 * LINE * samples * NZ * SLAB * 256, transcendentals=0, bytes_accessed=3 << 20
        ),
        name=f"pool_{k}",
    )(*operands)


def pair_kernel(place_ref, cot_ref, pooled_ref, out_ref):
    core = place_ref[0]
    ring = place_ref[1]
    samples = cot_ref.shape[0]

    def spots():
        for a in range(4):
            for b in range(4):
                line_at = jnp.where(core == 0, b, a)
                ring_at = jnp.where(core == 0, a, b)
                yield line_at, (ring_at - ring + 4) & 3

    spot_list = list(spots())
    for s in range(samples):
        pieces = [pooled_ref[line_at, s, k].astype(jnp.float32) for line_at, k in spot_list]
        wide = jnp.concatenate(pieces, axis=0)
        narrow = wide.astype(jnp.bfloat16)
        cot = cot_ref[s]
        total = jnp.dot(cot, narrow, preferred_element_type=jnp.float32)
        total = total + lax.dot_general(
            cot, narrow, (((0,), (0,)), ((), ())), preferred_element_type=jnp.float32
        )
        total = total + POOL_DECAY * wide
        for at, (line_at, k) in enumerate(spot_list):
            out_ref[line_at, s, k] = total[at * NZ : (at + 1) * NZ].astype(jnp.bfloat16)


def pair_rows(place, cotangent, pooled):
    samples = cotangent.shape[0]
    step = 8
    return pl.pallas_call(
        pair_kernel,
        out_shape=jax.ShapeDtypeStruct(pooled.shape, jnp.bfloat16),
        grid_spec=pltpu.PrefetchScalarGridSpec(
            num_scalar_prefetch=1,
            grid=(samples // step,),
            in_specs=[
                pl.BlockSpec((step, 128, 128), lambda i, place: (i, 0, 0)),
                pl.BlockSpec((LINE, step, 4, NZ, HALF), lambda i, place: (0, i, 0, 0, 0)),
            ],
            out_specs=pl.BlockSpec((LINE, step, 4, NZ, HALF), lambda i, place: (0, i, 0, 0, 0)),
        ),
        compiler_params=pltpu.CompilerParams(vmem_limit_bytes=48 << 20),
        cost_estimate=pl.CostEstimate(
            flops=4 * samples * 128 * 128 * 256, transcendentals=0, bytes_accessed=12 << 20
        ),
        name="pairwise",
    )(place, cotangent, pooled)


def spread_kernel(idx_low, idx_high, grads_ref, *rest):
    added = len(rest) == 5
    before_low, before_high = rest[:2] if added else (None, None)
    out_low, out_high, buffer = rest[-3:]
    rows = buffer.shape[0] // NZ
    step = pl.program_id(0)

    @pl.when(step == 0)
    def _():
        buffer[...] = grads_ref[...].reshape(rows * NZ, HALF).astype(jnp.float32)

    iota = lax.broadcasted_iota(jnp.int16, (SLAB, rows), 0)
    for idx_ref, before, out, shift in (
        (idx_low, before_low, out_low, 0),
        (idx_high, before_high, out_high, NZ // 2),
    ):
        grads = buffer[pl.ds(step + shift, rows, stride=NZ), :].astype(jnp.bfloat16)
        hits = counts_of([idx_ref[0, j : j + 1, :] for j in range(BAG)], iota)
        total = jnp.dot(hits, grads, preferred_element_type=jnp.float32)
        if added:
            total = total + before[0]
        out[0] = total


def spread_rows(k, idx, grads, previous):
    samples = grads.shape[1]
    rows = LINE * samples
    half = NZ // 2
    operands = [idx, idx, grads]
    in_specs = [
        pl.BlockSpec((1, BAG, rows), lambda i: (k * NZ + i, 0, 0)),
        pl.BlockSpec((1, BAG, rows), lambda i: (k * NZ + half + i, 0, 0)),
        pl.BlockSpec((LINE, samples, 1, NZ, HALF), lambda i: (0, 0, k, 0, 0)),
    ]
    out_spec = pl.BlockSpec((1, SLAB, HALF), lambda i: (i, 0, 0))
    aliases = {}
    if previous is not None:
        operands += list(previous)
        in_specs += [out_spec, out_spec]
        aliases = {3: 0, 4: 1}
    shape = jax.ShapeDtypeStruct((half, SLAB, HALF), jnp.float32)
    return pl.pallas_call(
        spread_kernel,
        out_shape=(shape, shape),
        grid=(half,),
        in_specs=in_specs,
        out_specs=(out_spec, out_spec),
        scratch_shapes=[pltpu.VMEM((rows * NZ, HALF), jnp.float32)],
        input_output_aliases=aliases,
        compiler_params=pltpu.CompilerParams(vmem_limit_bytes=48 << 20),
        cost_estimate=pl.CostEstimate(
            flops=2 * rows * NZ * SLAB * 256, transcendentals=0, bytes_accessed=6 << 20
        ),
        name=f"spread_{k}",
    )(*operands)


def dither_round(weights, dither_bits):
    magnitude = jnp.maximum(jnp.abs(weights), SMALLEST)
    spacing = jnp.exp2(jnp.floor(jnp.log2(magnitude)) - 7.0)
    grid_level = jnp.floor(weights / spacing + dither_bits.astype(jnp.float32) * DITHER_UNIT)
    return (grid_level * spacing).astype(jnp.bfloat16)


def adagrad_rows(slab_rows, grad_rows, state_rows, dither_bits):
    state_next = state_rows + jnp.mean(grad_rows * grad_rows, axis=-1)
    moved = (
        slab_rows.astype(jnp.float32)
        - LEARN_RATE * grad_rows / (jnp.sqrt(state_next) + 1e-08)[:, None]
    )
    return (dither_round(moved, dither_bits), state_next)


def per_device(
    lookup_block, lookup_offset, interaction_grad, table, adagrad_state, touched_blocks, dither
):
    core = lax.axis_index("rep")
    y = lax.axis_index("y")
    x = lax.axis_index("x")
    ring = jnp.where(core == 0, y, x)
    place = jnp.stack([core, ring]).astype(jnp.int32)
    row_count, emb_width = table.shape
    micro_count, sample_count = lookup_block.shape[:2]
    samples = micro_count * sample_count
    touch_count = touched_blocks.shape[1]

    table_blocks = table.reshape(row_count // BLOCK, BLOCK, emb_width)
    slab_table = table_blocks[touched_blocks[0]].reshape(SLAB, emb_width)
    own_half = lax.dynamic_slice(slab_table, (0, core * HALF), (SLAB, HALF))
    own_slabs = lax.all_gather(own_half, "z", axis=0, tiled=False)

    def flat(v):
        return v.transpose(0, 1, 3, 2).reshape(samples, 512).astype(jnp.bfloat16)

    own_lookups = jnp.concatenate([flat(lookup_block), flat(lookup_offset)], axis=1)
    both = jnp.concatenate([own_lookups, swap_cores(own_lookups)], axis=0)
    other_cot = swap_cores(interaction_grad)
    lane = lax.broadcasted_iota(jnp.int32, (512, 1), 0)
    bag_at = lane // 128
    y_at, x_at, z_at = (lane // 32) % 4, (lane // 8) % 4, lane % 8
    line_at = jnp.where(core == 0, x_at, y_at)
    ring_at = (jnp.where(core == 0, y_at, x_at) - ring + 4) % 4
    goes_to = line_at * 128 + ring_at * 32 + z_at * BAG + bag_at
    moves = goes_to == lax.broadcasted_iota(jnp.int32, (512, 512), 1)
    moves = jnp.concatenate([jnp.where(moves, 64.0, 0.0), jnp.where(moves, 1.0, 0.0)], axis=0)
    rows_out = jnp.dot(both, moves.astype(jnp.bfloat16), preferred_element_type=jnp.float32)
    rows_out = rows_out.reshape(2 * samples, LINE, 128).transpose(1, 0, 2)
    rows_in = line_exchange(rows_out).astype(jnp.int16)
    by_sample = [rows_in[:, c * samples : (c + 1) * samples] for c in range(2)]
    by_lookup = [
        v.astype(jnp.int32).reshape(LINE * samples, 128).T.astype(jnp.int16).reshape(
            32, BAG, LINE * samples
        )
        for v in by_sample
    ]

    from_left = ring_send(own_slabs, 1)
    from_right = ring_send(own_slabs, -1)
    across = jnp.concatenate(
        [ring_send(from_left[:4], 1), ring_send(from_right[4:], -1)], axis=0
    )
    slabs = {0: own_slabs, 1: from_right, 2: across, 3: from_left}

    cots = [
        interaction_grad.reshape(samples, 128, 128),
        other_cot.reshape(samples, 128, 128),
    ]
    pooled = [None, None]
    for k in (0, 3, 1, 2):
        for c in range(2):
            pooled[c] = pool_rows(k, by_sample[c], slabs[k], pooled[c])
    grads = []
    for c in range(2):
        arrived = line_exchange(pooled[c])
        grads.append(line_exchange(pair_rows(place, cots[c], arrived)))
    partial = {}
    for k in (2, 1, 3, 0):
        partial[k] = spread_rows(k, by_lookup[0], grads[0], None)
    for k in (2, 1, 3, 0):
        partial[k] = spread_rows(k, by_lookup[1], grads[1], partial[k])

    low_one = ring_send(partial[1][0] + ring_send(partial[2][0], 1), 1)
    high_three = ring_send(partial[3][1] + ring_send(partial[2][1], -1), -1)
    high_one = ring_send(partial[1][1], 1)
    low_three = ring_send(partial[3][0], -1)
    on_ring = jnp.concatenate(
        [partial[0][0] + low_one + low_three, partial[0][1] + high_one + high_three], axis=0
    )
    own_grad = lax.psum_scatter(on_ring, "z", scatter_dimension=0, tiled=True)[0]
    other_grad = swap_cores(own_grad)
    summed_grad = jnp.where(
        core == 0,
        jnp.concatenate([own_grad, other_grad], axis=1),
        jnp.concatenate([other_grad, own_grad], axis=1),
    )

    state_blocks = adagrad_state.reshape(row_count // BLOCK, BLOCK)
    state_slab = state_blocks[touched_blocks[0]].reshape(SLAB)
    new_rows, state_next = adagrad_rows(slab_table, summed_grad, state_slab, dither[0])
    updated_blocks = table_blocks.at[touched_blocks[0]].set(
        new_rows.reshape(touch_count, BLOCK, emb_width)
    )
    updated_state = state_blocks.at[touched_blocks[0]].set(state_next.reshape(touch_count, BLOCK))
    return (updated_blocks.reshape(row_count, emb_width), updated_state.reshape(row_count))


def solution(mesh):
    fine = Mesh(mesh.devices.reshape(2, NY, NX, NZ), AXES)
    tables = ("y", "x", "z")
    return jax.shard_map(
        per_device,
        mesh=fine,
        in_specs=(
            P(None, AXES, None, None),
            P(None, AXES, None, None),
            P(None, AXES, None, None),
            P(tables, None),
            P(tables),
            P(tables, None),
            P(tables, None, None),
        ),
        out_specs=(P(tables, None), P(tables)),
        check_vma=False,
    )
```

```python
import jax
import jax.numpy as jnp
from jax import lax
from jax.experimental import pallas as pl
from jax.experimental.pallas import tpu as pltpu
from jax.sharding import Mesh
from jax.sharding import PartitionSpec as P

BLOCK = 64
LEARN_RATE = 0.1
POOL_DECAY = 0.5
DITHER_UNIT = 2.0 ** (-15)
SMALLEST = 2.0 ** (-14)

NY, NX, NZ = 4, 4, 8
LINE = 4
HALF = 128
SLAB = 640
BAG = 4
AXES = ("rep", "y", "x", "z")


def device_id(r, y, x, z):
    return ((r * NY + y) * NX + x) * NZ + z


def moves_along(step_first, step_second):
    pairs = []
    for y in range(NY):
        for x in range(NX):
            for z in range(NZ):
                for core, (dy, dx, dz) in enumerate((step_first, step_second)):
                    to = device_id(core, (y + dy) % NY, (x + dx) % NX, (z + dz) % NZ)
                    pairs.append((device_id(core, y, x, z), to))
    return pairs


def ring_send(value, step):
    return lax.ppermute(value, AXES, moves_along((step, 0, 0), (0, step, 0)))


def line_send(value, step):
    return lax.ppermute(value, AXES, moves_along((0, step, 0), (step, 0, 0)))


def deep_send(value, step):
    return lax.ppermute(value, AXES, moves_along((0, 0, step), (0, 0, step)))


def swap_cores(value):
    return lax.ppermute(value, "rep", [(0, 1), (1, 0)])


def counts_of(columns, iota):
    one = jnp.ones((), jnp.bfloat16)
    zero = jnp.zeros((), jnp.bfloat16)
    total = None
    for column in columns:
        hit = jnp.where(column == iota, one, zero)
        total = hit if total is None else total + hit
    return total


def pool_kernel(k, place_ref, idx_ref, slab_ref, *rest):
    outs, buffer = rest[-5:-1], rest[-1]
    depth = place_ref[3]
    step = pl.program_id(0)
    rows = idx_ref.shape[1]
    idx = idx_ref[0]
    iota = lax.broadcasted_iota(jnp.int16, (rows, SLAB), 1)
    for i in range(NZ):
        base = k * 32 + i * BAG
        hits = counts_of([idx[:, base + j : base + j + 1] for j in range(BAG)], iota)
        rows_sum = jnp.dot(hits, slab_ref[i], preferred_element_type=jnp.float32)
        buffer[pl.ds((depth + i) & 7, rows, stride=NZ), :] = rows_sum
    for d in range(LINE):

        @pl.when(step == d)
        def _():
            outs[d][...] = buffer[...].astype(jnp.bfloat16).reshape(rows, 1, NZ, HALF)


def pool_rows(k, place, idx, slabs, previous):
    samples = idx.shape[1]
    operands = [idx, slabs]
    in_specs = [
        pl.BlockSpec((1, samples, 128), lambda i, place: (i, 0, 0)),
        pl.BlockSpec((NZ, SLAB, HALF), lambda i, place: (0, 0, 0)),
    ]
    aliases = {}
    if previous is not None:
        operands += list(previous)
        in_specs += [pl.BlockSpec(memory_space=pl.ANY)] * LINE
        aliases = {3 + d: d for d in range(LINE)}
    shape = jax.ShapeDtypeStruct((samples, 4, NZ, HALF), jnp.bfloat16)
    return pl.pallas_call(
        lambda *refs: pool_kernel(k, *refs),
        out_shape=(shape,) * LINE,
        grid_spec=pltpu.PrefetchScalarGridSpec(
            num_scalar_prefetch=1,
            grid=(LINE,),
            in_specs=in_specs,
            out_specs=(pl.BlockSpec((samples, 1, NZ, HALF), lambda i, place: (0, k, 0, 0)),) * LINE,
            scratch_shapes=[pltpu.VMEM((samples * NZ, HALF), jnp.float32)],
        ),
        input_output_aliases=aliases,
        compiler_params=pltpu.CompilerParams(vmem_limit_bytes=48 << 20),
        cost_estimate=pl.CostEstimate(
            flops=2 * LINE * samples * NZ * SLAB * 256, transcendentals=0, bytes_accessed=3 << 20
        ),
        name=f"pool_{k}",
    )(place, *operands)


def pair_kernel(place_ref, cot_ref, *rest):
    pooled, outs, (wide_ref, total_ref) = rest[:4], rest[4:8], rest[8:]
    core, ring, line = place_ref[0], place_ref[1], place_ref[2]
    samples = cot_ref.shape[0]

    def spot_of(d, k):
        line_at = (line - d + 4) & 3
        ring_at = (ring + k) & 3
        return jnp.where(core == 0, ring_at * 4 + line_at, line_at * 4 + ring_at)

    for d in range(LINE):
        for k in range(4):
            wide_ref[spot_of(d, k)] = pooled[d][:, k].astype(jnp.float32)
    for s in range(samples):
        wide = wide_ref[:, s].reshape(128, HALF)
        narrow = wide.astype(jnp.bfloat16)
        cot = cot_ref[s]
        total = jnp.dot(cot, narrow, preferred_element_type=jnp.float32)
        total = total + lax.dot_general(
            cot, narrow, (((0,), (0,)), ((), ())), preferred_element_type=jnp.float32
        )
        total = total + POOL_DECAY * wide
        total_ref[:, s] = total.reshape(16, NZ, HALF)
    for d in range(LINE):
        for k in range(4):
            outs[d][:, k] = total_ref[spot_of(d, k)].astype(jnp.bfloat16)


def pair_rows(place, cotangent, pooled):
    samples = cotangent.shape[0]
    step = 8
    spec = pl.BlockSpec((step, 4, NZ, HALF), lambda i, place: (i, 0, 0, 0))
    return pl.pallas_call(
        pair_kernel,
        out_shape=(jax.ShapeDtypeStruct(pooled[0].shape, jnp.bfloat16),) * LINE,
        grid_spec=pltpu.PrefetchScalarGridSpec(
            num_scalar_prefetch=1,
            grid=(samples // step,),
            in_specs=[pl.BlockSpec((step, 128, 128), lambda i, place: (i, 0, 0))] + [spec] * LINE,
            out_specs=(spec,) * LINE,
            scratch_shapes=[pltpu.VMEM((16, step, NZ, HALF), jnp.float32)] * 2,
        ),
        compiler_params=pltpu.CompilerParams(vmem_limit_bytes=48 << 20),
        cost_estimate=pl.CostEstimate(
            flops=4 * samples * 128 * 128 * 256, transcendentals=0, bytes_accessed=12 << 20
        ),
        name="pairwise",
    )(place, cotangent, *pooled)


def spread_kernel(place_ref, idx_low, idx_high, *rest):
    grads_refs = rest[:LINE]
    added = len(rest) == LINE + 5
    before_low, before_high = rest[LINE : LINE + 2] if added else (None, None)
    out_low, out_high, buffer = rest[-3:]
    rows = buffer.shape[0] // NZ
    part = buffer.shape[0] // LINE
    step = pl.program_id(0)
    depth = place_ref[3]

    @pl.when(step == 0)
    def _():
        for d in range(LINE):
            buffer[d * part : (d + 1) * part] = (
                grads_refs[d][...].reshape(part, HALF).astype(jnp.float32)
            )

    iota = lax.broadcasted_iota(jnp.int16, (SLAB, rows), 0)
    for idx_ref, before, out, shift in (
        (idx_low, before_low, out_low, 0),
        (idx_high, before_high, out_high, NZ // 2),
    ):
        at = (depth + step + shift) & 7
        grads = buffer[pl.ds(at, rows, stride=NZ), :].astype(jnp.bfloat16)
        hits = counts_of([idx_ref[0, j : j + 1, :] for j in range(BAG)], iota)
        total = jnp.dot(hits, grads, preferred_element_type=jnp.float32)
        if added:
            total = total + before[0]
        out[0] = total


def spread_rows(k, place, idx, grads, previous):
    samples = grads[0].shape[0]
    rows = LINE * samples
    half = NZ // 2
    operands = [idx, idx, *grads]
    in_specs = [
        pl.BlockSpec((1, BAG, rows), lambda i, place: (k * NZ + i, 0, 0)),
        pl.BlockSpec((1, BAG, rows), lambda i, place: (k * NZ + half + i, 0, 0)),
    ] + [pl.BlockSpec((samples, 1, NZ, HALF), lambda i, place: (0, k, 0, 0))] * LINE
    out_spec = pl.BlockSpec((1, SLAB, HALF), lambda i, place: (i, 0, 0))
    aliases = {}
    if previous is not None:
        operands += list(previous)
        in_specs += [out_spec, out_spec]
        aliases = {7: 0, 8: 1}
    shape = jax.ShapeDtypeStruct((half, SLAB, HALF), jnp.float32)
    return pl.pallas_call(
        spread_kernel,
        out_shape=(shape, shape),
        grid_spec=pltpu.PrefetchScalarGridSpec(
            num_scalar_prefetch=1,
            grid=(half,),
            in_specs=in_specs,
            out_specs=(out_spec, out_spec),
            scratch_shapes=[pltpu.VMEM((rows * NZ, HALF), jnp.float32)],
        ),
        input_output_aliases=aliases,
        compiler_params=pltpu.CompilerParams(vmem_limit_bytes=48 << 20),
        cost_estimate=pl.CostEstimate(
            flops=2 * rows * NZ * SLAB * 256, transcendentals=0, bytes_accessed=6 << 20
        ),
        name=f"spread_{k}",
    )(place, *operands)


def dither_round(weights, dither_bits):
    magnitude = jnp.maximum(jnp.abs(weights), SMALLEST)
    spacing = jnp.exp2(jnp.floor(jnp.log2(magnitude)) - 7.0)
    grid_level = jnp.floor(weights / spacing + dither_bits.astype(jnp.float32) * DITHER_UNIT)
    return (grid_level * spacing).astype(jnp.bfloat16)


def adagrad_rows(slab_rows, grad_rows, state_rows, dither_bits):
    state_next = state_rows + jnp.mean(grad_rows * grad_rows, axis=-1)
    moved = (
        slab_rows.astype(jnp.float32)
        - LEARN_RATE * grad_rows / (jnp.sqrt(state_next) + 1e-08)[:, None]
    )
    return (dither_round(moved, dither_bits), state_next)


def per_device(
    lookup_block, lookup_offset, interaction_grad, table, adagrad_state, touched_blocks, dither
):
    core = lax.axis_index("rep")
    y = lax.axis_index("y")
    x = lax.axis_index("x")
    depth = lax.axis_index("z")
    ring = jnp.where(core == 0, y, x)
    line = jnp.where(core == 0, x, y)
    place = jnp.stack([core, ring, line, depth]).astype(jnp.int32)
    row_count, emb_width = table.shape
    micro_count, sample_count = lookup_block.shape[:2]
    samples = micro_count * sample_count
    touch_count = touched_blocks.shape[1]

    def flat(v):
        return v.transpose(0, 1, 3, 2).reshape(samples, 512).astype(jnp.bfloat16)

    own_lookups = jnp.concatenate([flat(lookup_block), flat(lookup_offset)], axis=1)
    both = jnp.concatenate([own_lookups, swap_cores(own_lookups)], axis=0)
    other_cot = swap_cores(interaction_grad)
    lane = lax.broadcasted_iota(jnp.int32, (512, 1), 0)
    bag_at = lane // 128
    y_at, x_at, z_at = (lane // 32) % 4, (lane // 8) % 4, (lane - depth + 8) % 8
    line_at = (jnp.where(core == 0, x_at, y_at) - line + 4) % 4
    ring_at = (jnp.where(core == 0, y_at, x_at) - ring + 4) % 4
    goes_to = line_at * 128 + ring_at * 32 + z_at * BAG + bag_at
    moves = goes_to == lax.broadcasted_iota(jnp.int32, (512, 512), 1)
    moves = jnp.concatenate([jnp.where(moves, 64.0, 0.0), jnp.where(moves, 1.0, 0.0)], axis=0)
    rows_out = jnp.dot(both, moves.astype(jnp.bfloat16), preferred_element_type=jnp.float32)
    rows_in = jnp.stack(
        [rows_out[:, :128]]
        + [line_send(rows_out[:, 128 * (LINE - d) : 128 * (LINE - d + 1)], -d) for d in (1, 2, 3)]
    )
    by_sample = [rows_in[:, c * samples : (c + 1) * samples].astype(jnp.int16) for c in range(2)]
    by_lookup = [
        rows_in[:, c * samples : (c + 1) * samples]
        .reshape(LINE * samples, 128)
        .T.astype(jnp.int16)
        .reshape(32, BAG, LINE * samples)
        for c in range(2)
    ]

    table_blocks = table.reshape(row_count // BLOCK, BLOCK, emb_width)
    slab_table = table_blocks[touched_blocks[0]].reshape(SLAB, emb_width)
    own_half = lax.dynamic_slice(slab_table, (0, core * HALF), (SLAB, HALF))
    behind, ahead = [own_half], [own_half]
    for _ in range(3):
        behind.append(deep_send(behind[-1], 1))
        ahead.append(deep_send(ahead[-1], -1))
    middle = SLAB // 2
    opposite = jnp.concatenate(
        [deep_send(behind[3][:middle], 1), deep_send(ahead[3][middle:], -1)], axis=0
    )
    own_slabs = jnp.stack([*ahead, opposite, behind[3], behind[2], behind[1]])
    from_left = ring_send(own_slabs, 1)
    from_right = ring_send(own_slabs, -1)
    across = jnp.concatenate(
        [ring_send(from_left[:4], 1), ring_send(from_right[4:], -1)], axis=0
    )
    slabs = {0: own_slabs, 1: from_right, 2: across, 3: from_left}

    cots = [
        interaction_grad.reshape(samples, 128, 128),
        other_cot.reshape(samples, 128, 128),
    ]
    pooled = [None, None]
    for k in (0, 3, 1, 2):
        for c in range(2):
            pooled[c] = pool_rows(k, place, by_sample[c], slabs[k], pooled[c])
    grads = []
    for c in range(2):
        arrived = [pooled[c][0]] + [line_send(pooled[c][d], d) for d in (1, 2, 3)]
        paired = pair_rows(place, cots[c], arrived)
        grads.append([paired[0]] + [line_send(paired[d], -d) for d in (1, 2, 3)])
    partial = {}
    for k in (2, 1, 3, 0):
        partial[k] = spread_rows(k, place, by_lookup[0], grads[0], None)
    late, partial = lax.optimization_barrier((grads[1], partial))
    for k in (2, 1, 3, 0):
        partial[k] = spread_rows(k, place, by_lookup[1], late, partial[k])

    low_one = ring_send(partial[1][0] + ring_send(partial[2][0], 1), 1)
    high_three = ring_send(partial[3][1] + ring_send(partial[2][1], -1), -1)
    high_one = ring_send(partial[1][1], 1)
    low_three = ring_send(partial[3][0], -1)
    low = partial[0][0] + low_one + low_three
    high = partial[0][1] + high_one + high_three
    up = low[3] + jnp.pad(deep_send(high[0, :middle], 1), ((0, middle), (0, 0)))
    down = high[1] + jnp.pad(deep_send(high[0, middle:], -1), ((middle, 0), (0, 0)))
    for i in (2, 1, 0):
        up = deep_send(up, 1)
        down = deep_send(down, -1)
        if i:
            up = low[i] + up
            down = high[4 - i] + down
    own_grad = low[0] + up + down
    other_grad = swap_cores(own_grad)
    summed_grad = jnp.where(
        core == 0,
        jnp.concatenate([own_grad, other_grad], axis=1),
        jnp.concatenate([other_grad, own_grad], axis=1),
    )

    state_blocks = adagrad_state.reshape(row_count // BLOCK, BLOCK)
    state_slab = state_blocks[touched_blocks[0]].reshape(SLAB)
    new_rows, state_next = adagrad_rows(slab_table, summed_grad, state_slab, dither[0])
    updated_blocks = table_blocks.at[touched_blocks[0]].set(
        new_rows.reshape(touch_count, BLOCK, emb_width)
    )
    updated_state = state_blocks.at[touched_blocks[0]].set(state_next.reshape(touch_count, BLOCK))
    return (updated_blocks.reshape(row_count, emb_width), updated_state.reshape(row_count))


def solution(mesh):
    fine = Mesh(mesh.devices.reshape(2, NY, NX, NZ), AXES)
    tables = ("y", "x", "z")
    return jax.shard_map(
        per_device,
        mesh=fine,
        in_specs=(
            P(None, AXES, None, None),
            P(None, AXES, None, None),
            P(None, AXES, None, None),
            P(tables, None),
            P(tables),
            P(tables, None),
            P(tables, None, None),
        ),
        out_specs=(P(tables, None), P(tables)),
        check_vma=False,
    )
```

```python
import jax
import jax.numpy as jnp
from jax import lax
from jax.experimental import pallas as pl
from jax.experimental.pallas import tpu as pltpu
from jax.sharding import Mesh
from jax.sharding import PartitionSpec as P

BLOCK = 64
LEARN_RATE = 0.1
POOL_DECAY = 0.5
DITHER_UNIT = 2.0 ** (-15)
SMALLEST = 2.0 ** (-14)

NY, NX, NZ = 4, 4, 8
LINE = 4
HALF = 128
SLAB = 640
BAG = 4
AXES = ("rep", "y", "x", "z")


def device_id(r, y, x, z):
    return ((r * NY + y) * NX + x) * NZ + z


def moves_along(step_first, step_second):
    pairs = []
    for y in range(NY):
        for x in range(NX):
            for z in range(NZ):
                for core, (dy, dx, dz) in enumerate((step_first, step_second)):
                    to = device_id(core, (y + dy) % NY, (x + dx) % NX, (z + dz) % NZ)
                    pairs.append((device_id(core, y, x, z), to))
    return pairs


def ring_send(value, step):
    return lax.ppermute(value, AXES, moves_along((step, 0, 0), (0, step, 0)))


def line_send(value, step):
    return lax.ppermute(value, AXES, moves_along((0, step, 0), (step, 0, 0)))


def deep_send(value, step):
    return lax.ppermute(value, AXES, moves_along((0, 0, step), (0, 0, step)))


def swap_cores(value):
    return lax.ppermute(value, "rep", [(0, 1), (1, 0)])


def counts_of(columns, iota):
    one = jnp.ones((), jnp.bfloat16)
    zero = jnp.zeros((), jnp.bfloat16)
    total = None
    for column in columns:
        hit = jnp.where(column == iota, one, zero)
        total = hit if total is None else total + hit
    return total


def pool_kernel(k, place_ref, idx_ref, slab_ref, *rest):
    outs, buffer = rest[:LINE], rest[LINE]
    depth = place_ref[3]
    step = pl.program_id(0)
    rows = idx_ref.shape[1]
    idx = idx_ref[0]
    iota = lax.broadcasted_iota(jnp.int16, (rows, SLAB), 1)
    for i in range(NZ):
        base = k * 32 + i * BAG
        hits = counts_of([idx[:, base + j : base + j + 1] for j in range(BAG)], iota)
        rows_sum = jnp.dot(hits, slab_ref[i], preferred_element_type=jnp.float32)
        buffer[pl.ds((depth + i) & 7, rows, stride=NZ), :] = rows_sum
    for d in range(LINE):

        @pl.when(step == d)
        def _():
            outs[d][...] = buffer[...].astype(jnp.bfloat16).reshape(rows, NZ, HALF)


def pool_rows(k, place, idx, slabs):
    samples = idx.shape[1]
    shape = jax.ShapeDtypeStruct((samples, NZ, HALF), jnp.bfloat16)
    return pl.pallas_call(
        lambda *refs: pool_kernel(k, *refs),
        out_shape=(shape,) * LINE,
        grid_spec=pltpu.PrefetchScalarGridSpec(
            num_scalar_prefetch=1,
            grid=(LINE,),
            in_specs=[
                pl.BlockSpec((1, samples, 128), lambda i, place: (i, 0, 0)),
                pl.BlockSpec((NZ, SLAB, HALF), lambda i, place: (0, 0, 0)),
            ],
            out_specs=(pl.BlockSpec((samples, NZ, HALF), lambda i, place: (0, 0, 0)),) * LINE,
            scratch_shapes=[pltpu.VMEM((samples * NZ, HALF), jnp.float32)],
        ),
        compiler_params=pltpu.CompilerParams(vmem_limit_bytes=48 << 20),
        cost_estimate=pl.CostEstimate(
            flops=10**10, transcendentals=0, bytes_accessed=4 << 20
        ),
        name=f"pool_{k}",
    )(place, idx, slabs)


def pair_kernel(place_ref, cot_ref, *rest):
    pooled, outs, (wide_ref, total_ref) = rest[:16], rest[16:20], rest[20:]
    core, ring, line = place_ref[0], place_ref[1], place_ref[2]
    samples = cot_ref.shape[0]

    def spot_of(d, k):
        line_at = (line - d + 4) & 3
        ring_at = (ring + k) & 3
        return jnp.where(core == 0, ring_at * 4 + line_at, line_at * 4 + ring_at)

    for d in range(LINE):
        for k in range(4):
            wide_ref[spot_of(d, k)] = pooled[d * 4 + k][...].astype(jnp.float32)
    for s in range(samples):
        wide = wide_ref[:, s].reshape(128, HALF)
        narrow = wide.astype(jnp.bfloat16)
        cot = cot_ref[s]
        total = jnp.dot(cot, narrow, preferred_element_type=jnp.float32)
        total = total + lax.dot_general(
            cot, narrow, (((0,), (0,)), ((), ())), preferred_element_type=jnp.float32
        )
        total = total + POOL_DECAY * wide
        total_ref[:, s] = total.reshape(16, NZ, HALF)
    for d in range(LINE):
        for k in range(4):
            outs[d][:, k] = total_ref[spot_of(d, k)].astype(jnp.bfloat16)


def pair_rows(place, cotangent, pooled, first):
    samples = cotangent.shape[0]
    step = 32
    start = first // step
    taken = pl.BlockSpec((step, NZ, HALF), lambda i, place: (start + i, 0, 0))
    given = pl.BlockSpec((step, 4, NZ, HALF), lambda i, place: (i, 0, 0, 0))
    shape = jax.ShapeDtypeStruct((samples, 4, NZ, HALF), jnp.bfloat16)
    return pl.pallas_call(
        pair_kernel,
        out_shape=(shape,) * LINE,
        grid_spec=pltpu.PrefetchScalarGridSpec(
            num_scalar_prefetch=1,
            grid=(samples // step,),
            in_specs=[pl.BlockSpec((step, 128, 128), lambda i, place: (i, 0, 0))] + [taken] * 16,
            out_specs=(given,) * LINE,
            scratch_shapes=[pltpu.VMEM((16, step, NZ, HALF), jnp.float32)] * 2,
        ),
        compiler_params=pltpu.CompilerParams(vmem_limit_bytes=48 << 20),
        cost_estimate=pl.CostEstimate(
            flops=10**10, transcendentals=0, bytes_accessed=12 << 20
        ),
        name="pairwise",
    )(place, cotangent, *pooled)


def spread_kernel(place_ref, idx_low, idx_high, *rest):
    grads_refs = rest[:LINE]
    added = len(rest) == LINE + 5
    before_low, before_high = rest[LINE : LINE + 2] if added else (None, None)
    out_low, out_high, buffer = rest[-3:]
    rows = buffer.shape[0] // NZ
    part = buffer.shape[0] // LINE
    step = pl.program_id(0)
    depth = place_ref[3]

    @pl.when(step == 0)
    def _():
        for d in range(LINE):
            buffer[d * part : (d + 1) * part] = (
                grads_refs[d][...].reshape(part, HALF).astype(jnp.float32)
            )

    iota = lax.broadcasted_iota(jnp.int16, (SLAB, rows), 0)
    for idx_ref, before, out, shift in (
        (idx_low, before_low, out_low, 0),
        (idx_high, before_high, out_high, NZ // 2),
    ):
        at = (depth + step + shift) & 7
        grads = buffer[pl.ds(at, rows, stride=NZ), :].astype(jnp.bfloat16)
        hits = counts_of([idx_ref[0, j : j + 1, :] for j in range(BAG)], iota)
        total = jnp.dot(hits, grads, preferred_element_type=jnp.float32)
        if added:
            total = total + before[0]
        out[0] = total


def spread_rows(k, place, idx, grads, previous):
    samples = grads[0].shape[0]
    rows = LINE * samples
    half = NZ // 2
    operands = [idx, idx, *grads]
    in_specs = [
        pl.BlockSpec((1, BAG, rows), lambda i, place: (k * NZ + i, 0, 0)),
        pl.BlockSpec((1, BAG, rows), lambda i, place: (k * NZ + half + i, 0, 0)),
    ] + [pl.BlockSpec((samples, 1, NZ, HALF), lambda i, place: (0, k, 0, 0))] * LINE
    out_spec = pl.BlockSpec((1, SLAB, HALF), lambda i, place: (i, 0, 0))
    aliases = {}
    if previous is not None:
        operands += list(previous)
        in_specs += [out_spec, out_spec]
        aliases = {7: 0, 8: 1}
    shape = jax.ShapeDtypeStruct((half, SLAB, HALF), jnp.float32)
    return pl.pallas_call(
        spread_kernel,
        out_shape=(shape, shape),
        grid_spec=pltpu.PrefetchScalarGridSpec(
            num_scalar_prefetch=1,
            grid=(half,),
            in_specs=in_specs,
            out_specs=(out_spec, out_spec),
            scratch_shapes=[pltpu.VMEM((rows * NZ, HALF), jnp.float32)],
        ),
        input_output_aliases=aliases,
        compiler_params=pltpu.CompilerParams(vmem_limit_bytes=48 << 20),
        cost_estimate=pl.CostEstimate(
            flops=6 * 10**9, transcendentals=0, bytes_accessed=6 << 20
        ),
        name=f"spread_{k}",
    )(place, *operands)


def dither_round(weights, dither_bits):
    magnitude = jnp.maximum(jnp.abs(weights), SMALLEST)
    spacing = jnp.exp2(jnp.floor(jnp.log2(magnitude)) - 7.0)
    grid_level = jnp.floor(weights / spacing + dither_bits.astype(jnp.float32) * DITHER_UNIT)
    return (grid_level * spacing).astype(jnp.bfloat16)


def adagrad_rows(slab_rows, grad_rows, state_rows, dither_bits):
    state_next = state_rows + jnp.mean(grad_rows * grad_rows, axis=-1)
    moved = (
        slab_rows.astype(jnp.float32)
        - LEARN_RATE * grad_rows / (jnp.sqrt(state_next) + 1e-08)[:, None]
    )
    return (dither_round(moved, dither_bits), state_next)


def per_device(
    lookup_block, lookup_offset, interaction_grad, table, adagrad_state, touched_blocks, dither
):
    core = lax.axis_index("rep")
    y = lax.axis_index("y")
    x = lax.axis_index("x")
    depth = lax.axis_index("z")
    ring = jnp.where(core == 0, y, x)
    line = jnp.where(core == 0, x, y)
    place = jnp.stack([core, ring, line, depth]).astype(jnp.int32)
    row_count, emb_width = table.shape
    micro_count, sample_count = lookup_block.shape[:2]
    samples = micro_count * sample_count
    touch_count = touched_blocks.shape[1]

    table_blocks = table.reshape(row_count // BLOCK, BLOCK, emb_width)
    slab_table = table_blocks[touched_blocks[0]].reshape(SLAB, emb_width)
    own_half = lax.dynamic_slice(slab_table, (0, core * HALF), (SLAB, HALF))
    near = {i: deep_send(own_half, -i) for i in (1, 2)}
    near.update({8 - i: deep_send(own_half, i) for i in (1, 2)})

    def flat(v):
        return v.transpose(0, 1, 3, 2).reshape(samples, 512).astype(jnp.bfloat16)

    own_lookups = jnp.concatenate([flat(lookup_block), flat(lookup_offset)], axis=1)
    both = jnp.concatenate([own_lookups, swap_cores(own_lookups)], axis=0)
    other_cot = swap_cores(interaction_grad)
    lane = lax.broadcasted_iota(jnp.int32, (512, 1), 0)
    bag_at = lane // 128
    y_at, x_at, z_at = (lane // 32) % 4, (lane // 8) % 4, (lane - depth + 8) % 8
    line_at = (jnp.where(core == 0, x_at, y_at) - line + 4) % 4
    ring_at = (jnp.where(core == 0, y_at, x_at) - ring + 4) % 4
    goes_to = line_at * 128 + ring_at * 32 + z_at * BAG + bag_at
    moves = goes_to == lax.broadcasted_iota(jnp.int32, (512, 512), 1)
    moves = jnp.concatenate([jnp.where(moves, 64.0, 0.0), jnp.where(moves, 1.0, 0.0)], axis=0)
    rows_out = jnp.dot(both, moves.astype(jnp.bfloat16), preferred_element_type=jnp.float32)
    rows_out, near = lax.optimization_barrier((rows_out, near))
    rows_in = jnp.stack(
        [rows_out[:, :128]]
        + [line_send(rows_out[:, 128 * (LINE - d) : 128 * (LINE - d + 1)], -d) for d in (1, 2, 3)]
    )
    by_place = rows_in.astype(jnp.int16)
    by_lookup = [
        rows_in[:, c * samples : (c + 1) * samples]
        .reshape(LINE * samples, 128)
        .T.astype(jnp.int16)
        .reshape(32, BAG, LINE * samples)
        for c in range(2)
    ]

    middle = SLAB // 2
    opposite = jnp.concatenate(
        [deep_send(near[6][:middle], 2), deep_send(near[2][middle:], -2)], axis=0
    )
    own_slabs = jnp.stack(
        [
            own_half,
            near[1],
            near[2],
            deep_send(near[2], -1),
            opposite,
            deep_send(near[6], 1),
            near[6],
            near[7],
        ]
    )
    from_left = ring_send(own_slabs, 1)
    from_right = ring_send(own_slabs, -1)
    across = jnp.concatenate(
        [ring_send(from_left[:4], 1), ring_send(from_right[4:], -1)], axis=0
    )
    slabs = {0: own_slabs, 1: from_right, 2: across, 3: from_left}

    cots = [
        interaction_grad.reshape(samples, 128, 128),
        other_cot.reshape(samples, 128, 128),
    ]
    arrived = {}
    for k in (0, 3, 1, 2):
        pooled = pool_rows(k, place, by_place, slabs[k])
        for d in range(LINE):
            arrived[d, k] = line_send(pooled[d], d) if d else pooled[d]
    arrived = [arrived[d, k] for d in range(LINE) for k in range(4)]
    grads = []
    for c in range(2):
        paired = pair_rows(place, cots[c], arrived, c * samples)
        grads.append([paired[0]] + [line_send(paired[d], -d) for d in (1, 2, 3)])
    partial = {}
    for k in (2, 1, 3, 0):
        partial[k] = spread_rows(k, place, by_lookup[0], grads[0], None)
    late, partial = lax.optimization_barrier((grads[1], partial))
    for k in (2, 1, 3, 0):
        partial[k] = spread_rows(k, place, by_lookup[1], late, partial[k])

    low_one = ring_send(partial[1][0] + ring_send(partial[2][0], 1), 1)
    high_three = ring_send(partial[3][1] + ring_send(partial[2][1], -1), -1)
    high_one = ring_send(partial[1][1], 1)
    low_three = ring_send(partial[3][0], -1)
    low = partial[0][0] + low_one + low_three
    high = partial[0][1] + high_one + high_three
    up = low[3] + jnp.pad(deep_send(high[0, :middle], 1), ((0, middle), (0, 0)))
    down = high[1] + jnp.pad(deep_send(high[0, middle:], -1), ((middle, 0), (0, 0)))
    for i in (2, 1, 0):
        up = deep_send(up, 1)
        down = deep_send(down, -1)
        if i:
            up = low[i] + up
            down = high[4 - i] + down
    own_grad = low[0] + up + down
    other_grad = swap_cores(own_grad)
    summed_grad = jnp.where(
        core == 0,
        jnp.concatenate([own_grad, other_grad], axis=1),
        jnp.concatenate([other_grad, own_grad], axis=1),
    )

    state_blocks = adagrad_state.reshape(row_count // BLOCK, BLOCK)
    state_slab = state_blocks[touched_blocks[0]].reshape(SLAB)
    new_rows, state_next = adagrad_rows(slab_table, summed_grad, state_slab, dither[0])
    updated_blocks = table_blocks.at[touched_blocks[0]].set(
        new_rows.reshape(touch_count, BLOCK, emb_width)
    )
    updated_state = state_blocks.at[touched_blocks[0]].set(state_next.reshape(touch_count, BLOCK))
    return (updated_blocks.reshape(row_count, emb_width), updated_state.reshape(row_count))


def solution(mesh):
    fine = Mesh(mesh.devices.reshape(2, NY, NX, NZ), AXES)
    tables = ("y", "x", "z")
    return jax.shard_map(
        per_device,
        mesh=fine,
        in_specs=(
            P(None, AXES, None, None),
            P(None, AXES, None, None),
            P(None, AXES, None, None),
            P(tables, None),
            P(tables),
            P(tables, None),
            P(tables, None, None),
        ),
        out_specs=(P(tables, None), P(tables)),
        check_vma=False,
    )
```

```python
import jax
import jax.numpy as jnp
from jax import lax
from jax.experimental import pallas as pl
from jax.experimental.pallas import tpu as pltpu
from jax.sharding import Mesh
from jax.sharding import PartitionSpec as P

BLOCK = 64
LEARN_RATE = 0.1
POOL_DECAY = 0.5
DITHER_UNIT = 2.0 ** (-15)
SMALLEST = 2.0 ** (-14)

NY, NX, NZ = 4, 4, 8
LINE = 4
HALF = 128
SLAB = 640
BAG = 4
AXES = ("rep", "y", "x", "z")


def device_id(r, y, x, z):
    return ((r * NY + y) * NX + x) * NZ + z


def moves_along(step_first, step_second):
    pairs = []
    for y in range(NY):
        for x in range(NX):
            for z in range(NZ):
                for core, (dy, dx, dz) in enumerate((step_first, step_second)):
                    to = device_id(core, (y + dy) % NY, (x + dx) % NX, (z + dz) % NZ)
                    pairs.append((device_id(core, y, x, z), to))
    return pairs


def ring_send(value, step):
    return lax.ppermute(value, AXES, moves_along((step, 0, 0), (0, step, 0)))


def line_exchange(value):
    first = [[device_id(0, y, x, z) for x in range(NX)] for y in range(NY) for z in range(NZ)]
    second = [[device_id(1, y, x, z) for y in range(NY)] for x in range(NX) for z in range(NZ)]
    return lax.all_to_all(value, AXES, 0, 0, tiled=True, axis_index_groups=first + second)


def deep_send(value, step):
    return lax.ppermute(value, AXES, moves_along((0, 0, step), (0, 0, step)))


def swap_cores(value):
    return lax.ppermute(value, "rep", [(0, 1), (1, 0)])


def counts_of(columns, iota):
    one = jnp.ones((), jnp.bfloat16)
    zero = jnp.zeros((), jnp.bfloat16)
    total = None
    for column in columns:
        hit = jnp.where(column == iota, one, zero)
        total = hit if total is None else total + hit
    return total


def pool_kernel(k, place_ref, idx_ref, slab_ref, *rest):
    out_ref, buffer = rest[-2:]
    depth = place_ref[3]
    samples = idx_ref.shape[1]
    part = 128
    iota = lax.broadcasted_iota(jnp.int16, (part, SLAB), 1)

    def some_rows(at, carry):
        first = pl.multiple_of(at * part, part)
        idx = idx_ref[0, pl.ds(first, part), :]
        for i in range(NZ):
            base = k * 32 + i * BAG
            hits = counts_of([idx[:, base + j : base + j + 1] for j in range(BAG)], iota)
            rows_sum = jnp.dot(hits, slab_ref[i], preferred_element_type=jnp.float32)
            buffer[pl.ds(first * NZ + ((depth + i) & 7), part, stride=NZ), :] = rows_sum
        return carry

    lax.fori_loop(0, samples // part, some_rows, 0)
    out_ref[...] = buffer[...].astype(jnp.bfloat16).reshape(1, samples, 1, NZ, HALF)


def pool_rows(k, place, idx, slabs, slot, slots, previous):
    samples = idx.shape[1]
    operands = [idx, slabs]
    in_specs = [
        pl.BlockSpec((1, samples, 128), lambda i, place: (i, 0, 0)),
        pl.BlockSpec((NZ, SLAB, HALF), lambda i, place: (0, 0, 0)),
    ]
    aliases = {}
    if previous is not None:
        operands.append(previous)
        in_specs.append(pl.BlockSpec(memory_space=pl.ANY))
        aliases = {3: 0}
    return pl.pallas_call(
        lambda *refs: pool_kernel(k, *refs),
        out_shape=jax.ShapeDtypeStruct((LINE, samples, slots, NZ, HALF), jnp.bfloat16),
        grid_spec=pltpu.PrefetchScalarGridSpec(
            num_scalar_prefetch=1,
            grid=(LINE,),
            in_specs=in_specs,
            out_specs=pl.BlockSpec((1, samples, 1, NZ, HALF), lambda i, place: (i, 0, slot, 0, 0)),
            scratch_shapes=[pltpu.VMEM((samples * NZ, HALF), jnp.float32)],
        ),
        input_output_aliases=aliases,
        compiler_params=pltpu.CompilerParams(vmem_limit_bytes=48 << 20),
        cost_estimate=pl.CostEstimate(flops=3*10**9, transcendentals=0, bytes_accessed=4 << 20),
        name=f"pool_{k}",
    )(place, *operands)


PLACES = ((0,), (3,), (1, 2))


def pair_kernel(place_ref, cot_ref, *rest):
    pooled, out_ref, (wide_ref, total_ref) = rest[: len(PLACES)], rest[-3], rest[-2:]
    core, ring = place_ref[0], place_ref[1]
    samples = cot_ref.shape[0]

    def spot_of(line_at, k):
        ring_at = (ring + k) & 3
        return jnp.where(core == 0, ring_at * 4 + line_at, line_at * 4 + ring_at)

    for ks, ref in zip(PLACES, pooled):
        for slot, k in enumerate(ks):
            for line_at in range(LINE):
                wide_ref[spot_of(line_at, k)] = ref[line_at, :, slot].astype(jnp.float32)
    together = 8

    def some_samples(at, carry):
        for s in range(together):
            sample = at * together + s
            wide = wide_ref[:, sample].reshape(128, HALF)
            narrow = wide.astype(jnp.bfloat16)
            cot = cot_ref[sample]
            total = jnp.dot(cot, narrow, preferred_element_type=jnp.float32)
            total = total + lax.dot_general(
                cot, narrow, (((0,), (0,)), ((), ())), preferred_element_type=jnp.float32
            )
            total = total + POOL_DECAY * wide
            total_ref[:, sample] = total.reshape(16, NZ, HALF)
        return carry

    lax.fori_loop(0, samples // together, some_samples, 0)
    for line_at in range(LINE):
        for k in range(4):
            out_ref[line_at, :, k] = total_ref[spot_of(line_at, k)].astype(jnp.bfloat16)


def pair_rows(place, cotangent, pooled, first):
    samples = cotangent.shape[0]
    step = 32
    start = first // step
    taken = [
        pl.BlockSpec((LINE, step, len(ks), NZ, HALF), lambda i, place: (0, start + i, 0, 0, 0))
        for ks in PLACES
    ]
    return pl.pallas_call(
        pair_kernel,
        out_shape=jax.ShapeDtypeStruct((LINE, samples, 4, NZ, HALF), jnp.bfloat16),
        grid_spec=pltpu.PrefetchScalarGridSpec(
            num_scalar_prefetch=1,
            grid=(samples // step,),
            in_specs=[pl.BlockSpec((step, 128, 128), lambda i, place: (i, 0, 0))] + taken,
            out_specs=pl.BlockSpec((LINE, step, 4, NZ, HALF), lambda i, place: (0, i, 0, 0, 0)),
            scratch_shapes=[pltpu.VMEM((16, step, NZ, HALF), jnp.float32)] * 2,
        ),
        compiler_params=pltpu.CompilerParams(vmem_limit_bytes=48 << 20),
        cost_estimate=pl.CostEstimate(flops=10**9, transcendentals=0, bytes_accessed=12 << 20),
        name="pairwise",
    )(place, cotangent, *pooled)


def spread_kernel(places, place_ref, idx_low, idx_high, grads_ref, *rest):
    out_low, out_high, buffer = rest[-3:]
    before_low, before_high = rest[:2] if len(rest) == 5 else (None, None)
    rows = buffer.shape[0] // NZ
    step = pl.program_id(0) & 3

    @pl.when(step == 0)
    def _():
        buffer[...] = grads_ref[...].reshape(rows * NZ, HALF).astype(jnp.float32)

    iota = lax.broadcasted_iota(jnp.int16, (SLAB, rows), 0)
    for idx_ref, before, out, shift in (
        (idx_low, before_low, out_low, 0),
        (idx_high, before_high, out_high, NZ // 2),
    ):
        grads = buffer[pl.ds(step + shift, rows, stride=NZ), :].astype(jnp.bfloat16)
        hits = counts_of([idx_ref[0, j : j + 1, :] for j in range(BAG)], iota)
        total = jnp.dot(hits, grads, preferred_element_type=jnp.float32)
        if before is not None:
            total = total + before[0, 0]
        out[0, 0] = total


def spread_rows(first, places, place, idx, grads, previous):
    samples = grads.shape[1]
    rows = LINE * samples
    half = NZ // 2

    def lookups(shift):
        def at(i, place):
            k = first + (i >> 2)
            return (k * NZ + (((i & 3) + shift - place[3]) & 7), 0, 0)

        return pl.BlockSpec((1, BAG, rows), at)

    operands = [idx, idx, grads]
    in_specs = [
        lookups(0),
        lookups(half),
        pl.BlockSpec(
            (LINE, samples, 1, NZ, HALF), lambda i, place: (0, 0, first + (i >> 2), 0, 0)
        ),
    ]
    if previous is not None:
        operands += list(previous)
        in_specs += [
            pl.BlockSpec((1, 1, SLAB, HALF), lambda i, place: (first + (i >> 2), i & 3, 0, 0))
        ] * 2
    shape = jax.ShapeDtypeStruct((places, half, SLAB, HALF), jnp.float32)
    return pl.pallas_call(
        lambda *refs: spread_kernel(places, *refs),
        out_shape=(shape, shape),
        grid_spec=pltpu.PrefetchScalarGridSpec(
            num_scalar_prefetch=1,
            grid=(places * half,),
            in_specs=in_specs,
            out_specs=(
                pl.BlockSpec((1, 1, SLAB, HALF), lambda i, place: (i >> 2, i & 3, 0, 0)),
            )
            * 2,
            scratch_shapes=[pltpu.VMEM((rows * NZ, HALF), jnp.float32)],
        ),
        compiler_params=pltpu.CompilerParams(vmem_limit_bytes=48 << 20),
        cost_estimate=pl.CostEstimate(
            flops=places * 10**9, transcendentals=0, bytes_accessed=places * 6 << 20
        ),
        name=f"spread_{first}",
    )(place, *operands)


def dither_round(weights, dither_bits):
    magnitude = jnp.maximum(jnp.abs(weights), SMALLEST)
    spacing = jnp.exp2(jnp.floor(jnp.log2(magnitude)) - 7.0)
    grid_level = jnp.floor(weights / spacing + dither_bits.astype(jnp.float32) * DITHER_UNIT)
    return (grid_level * spacing).astype(jnp.bfloat16)


def adagrad_rows(slab_rows, grad_rows, state_rows, dither_bits):
    state_next = state_rows + jnp.mean(grad_rows * grad_rows, axis=-1)
    moved = (
        slab_rows.astype(jnp.float32)
        - LEARN_RATE * grad_rows / (jnp.sqrt(state_next) + 1e-08)[:, None]
    )
    return (dither_round(moved, dither_bits), state_next)


def per_device(
    lookup_block, lookup_offset, interaction_grad, table, adagrad_state, touched_blocks, dither
):
    core = lax.axis_index("rep")
    y = lax.axis_index("y")
    x = lax.axis_index("x")
    depth = lax.axis_index("z")
    ring = jnp.where(core == 0, y, x)
    line = jnp.where(core == 0, x, y)
    place = jnp.stack([core, ring, line, depth]).astype(jnp.int32)
    row_count, emb_width = table.shape
    micro_count, sample_count = lookup_block.shape[:2]
    samples = micro_count * sample_count
    touch_count = touched_blocks.shape[1]

    table_blocks = table.reshape(row_count // BLOCK, BLOCK, emb_width)
    slab_table = table_blocks[touched_blocks[0]].reshape(SLAB, emb_width)
    own_half = lax.dynamic_slice(slab_table, (0, core * HALF), (SLAB, HALF))
    def flat(v):
        return v.transpose(0, 1, 3, 2).reshape(samples, 512).astype(jnp.bfloat16)

    own_lookups = jnp.concatenate([flat(lookup_block), flat(lookup_offset)], axis=1)
    both = jnp.concatenate([own_lookups, swap_cores(own_lookups)], axis=0)
    lane = lax.broadcasted_iota(jnp.int32, (512, 1), 0)
    bag_at = lane // 128
    y_at, x_at, z_at = (lane // 32) % 4, (lane // 8) % 4, (lane - depth + 8) % 8
    line_at = jnp.where(core == 0, x_at, y_at)
    ring_at = (jnp.where(core == 0, y_at, x_at) - ring + 4) % 4
    goes_to = line_at * 128 + ring_at * 32 + z_at * BAG + bag_at
    moves = goes_to == lax.broadcasted_iota(jnp.int32, (512, 512), 1)
    moves = jnp.concatenate([jnp.where(moves, 64.0, 0.0), jnp.where(moves, 1.0, 0.0)], axis=0)
    rows_out = jnp.dot(both, moves.astype(jnp.bfloat16), preferred_element_type=jnp.float32)
    rows_out = jnp.stack([rows_out[:, 128 * at : 128 * (at + 1)] for at in range(LINE)])

    near = {i: deep_send(own_half, -i) for i in (1, 2)}
    near.update({8 - i: deep_send(own_half, i) for i in (1, 2)})
    rows_in = line_exchange(rows_out)
    again, _ = lax.optimization_barrier((own_half, rows_out))
    far = {3: deep_send(again, -3), 5: deep_send(again, 3), 4: deep_send(again, 4)}
    deep = {0: own_half, **near, **far}
    own_slabs = jnp.stack([deep[i] for i in range(NZ)])
    slabs = {0: own_slabs, 1: ring_send(own_slabs, -1), 3: ring_send(own_slabs, 1)}
    again, _ = lax.optimization_barrier((own_slabs, slabs))
    slabs[2] = ring_send(again, 2)
    other_cot = swap_cores(interaction_grad)
    by_place = rows_in.astype(jnp.int16)
    by_lookup = [
        rows_in[:, c * samples : (c + 1) * samples]
        .reshape(LINE * samples, 128)
        .T.astype(jnp.int16)
        .reshape(32, BAG, LINE * samples)
        for c in range(2)
    ]

    cots = [
        interaction_grad.reshape(samples, 128, 128),
        other_cot.reshape(samples, 128, 128),
    ]
    arrived = []
    for ks in PLACES:
        pooled = None
        for slot, k in enumerate(ks):
            pooled = pool_rows(k, place, by_place, slabs[k], slot, len(ks), pooled)
        arrived.append(line_exchange(pooled))
    paired = [pair_rows(place, cots[c], arrived, c * samples) for c in range(2)]
    grads = [line_exchange(v) for v in paired]
    early, _ = lax.optimization_barrier((grads[0], paired[1]))
    before = spread_rows(0, 4, place, by_lookup[0], early, None)
    late, before = lax.optimization_barrier((grads[1], before))
    low, high = {}, {}
    for k in (2, 1, 3, 0):
        low[k], high[k] = spread_rows(k, 1, place, by_lookup[1], late, before)

    low_one = ring_send(low[1] + ring_send(low[2], 1), 1)
    high_three = ring_send(high[3] + ring_send(high[2], -1), -1)
    high_one = ring_send(high[1], 1)
    low_three = ring_send(low[3], -1)
    on_ring = jnp.concatenate([low[0] + low_one + low_three, high[0] + high_one + high_three], axis=1)
    own_grad = lax.psum_scatter(on_ring[0], "z", scatter_dimension=0, tiled=True)[0]
    other_grad = swap_cores(own_grad)
    summed_grad = jnp.where(
        core == 0,
        jnp.concatenate([own_grad, other_grad], axis=1),
        jnp.concatenate([other_grad, own_grad], axis=1),
    )

    state_blocks = adagrad_state.reshape(row_count // BLOCK, BLOCK)
    state_slab = state_blocks[touched_blocks[0]].reshape(SLAB)
    new_rows, state_next = adagrad_rows(slab_table, summed_grad, state_slab, dither[0])
    updated_blocks = table_blocks.at[touched_blocks[0]].set(
        new_rows.reshape(touch_count, BLOCK, emb_width)
    )
    updated_state = state_blocks.at[touched_blocks[0]].set(state_next.reshape(touch_count, BLOCK))
    return (updated_blocks.reshape(row_count, emb_width), updated_state.reshape(row_count))


def solution(mesh):
    fine = Mesh(mesh.devices.reshape(2, NY, NX, NZ), AXES)
    tables = ("y", "x", "z")
    return jax.shard_map(
        per_device,
        mesh=fine,
        in_specs=(
            P(None, AXES, None, None),
            P(None, AXES, None, None),
            P(None, AXES, None, None),
            P(tables, None),
            P(tables),
            P(tables, None),
            P(tables, None, None),
        ),
        out_specs=(P(tables, None), P(tables)),
        check_vma=False,
    )
```

```python
import jax
import jax.numpy as jnp
from jax import lax
from jax.experimental import pallas as pl
from jax.experimental.pallas import tpu as pltpu
from jax.sharding import Mesh
from jax.sharding import PartitionSpec as P

BLOCK = 64
LEARN_RATE = 0.1
POOL_DECAY = 0.5
DITHER_UNIT = 2.0 ** (-15)
SMALLEST = 2.0 ** (-14)

NY, NX, NZ = 4, 4, 8
LINE = 4
HALF = 128
SLAB = 640
BAG = 4
AXES = ("rep", "y", "x", "z")


def device_id(r, y, x, z):
    return ((r * NY + y) * NX + x) * NZ + z


def moves_along(step_first, step_second):
    pairs = []
    for y in range(NY):
        for x in range(NX):
            for z in range(NZ):
                for core, (dy, dx, dz) in enumerate((step_first, step_second)):
                    to = device_id(core, (y + dy) % NY, (x + dx) % NX, (z + dz) % NZ)
                    pairs.append((device_id(core, y, x, z), to))
    return pairs


def ring_send(value, step):
    return lax.ppermute(value, AXES, moves_along((step, 0, 0), (0, step, 0)))


def line_send(value, step):
    return lax.ppermute(value, AXES, moves_along((0, step, 0), (step, 0, 0)))


def deep_send(value, step):
    return lax.ppermute(value, AXES, moves_along((0, 0, step), (0, 0, step)))


def swap_cores(value):
    return lax.ppermute(value, "rep", [(0, 1), (1, 0)])


def counts_of(columns, iota):
    one = jnp.ones((), jnp.bfloat16)
    zero = jnp.zeros((), jnp.bfloat16)
    total = None
    for column in columns:
        hit = jnp.where(column == iota, one, zero)
        total = hit if total is None else total + hit
    return total


def pool_kernel(k, place_ref, idx_ref, slab_ref, *rest):
    outs, buffer = rest[-LINE - 1 : -1], rest[-1]
    depth = place_ref[3]
    step = pl.program_id(0)
    chips, samples = idx_ref.shape[:2]
    rows = chips * samples
    idx = idx_ref[...].reshape(rows, 128)
    iota = lax.broadcasted_iota(jnp.int16, (rows, SLAB), 1)
    for i in range(NZ):
        base = k * 32 + i * BAG
        hits = counts_of([idx[:, base + j : base + j + 1] for j in range(BAG)], iota)
        rows_sum = jnp.dot(hits, slab_ref[i], preferred_element_type=jnp.float32)
        buffer[pl.ds((depth + i) & 7, rows, stride=NZ), :] = rows_sum
    for d in range(LINE):
        first = (d % chips) * samples * NZ

        @pl.when(step == d // chips)
        def _():
            outs[d][...] = (
                buffer[first : first + samples * NZ]
                .astype(jnp.bfloat16)
                .reshape(samples, 1, NZ, HALF)
            )


def pool_rows(k, place, idx, slabs, previous):
    samples = idx.shape[1]
    chips = 2
    operands = [idx, slabs]
    in_specs = [
        pl.BlockSpec((chips, samples, 128), lambda i, place: (i, 0, 0)),
        pl.BlockSpec((NZ, SLAB, HALF), lambda i, place: (0, 0, 0)),
    ]
    aliases = {}
    if previous is not None:
        operands += list(previous)
        in_specs += [pl.BlockSpec(memory_space=pl.ANY)] * LINE
        aliases = {3 + d: d for d in range(LINE)}
    shape = jax.ShapeDtypeStruct((samples, 4, NZ, HALF), jnp.bfloat16)
    return pl.pallas_call(
        lambda *refs: pool_kernel(k, *refs),
        out_shape=(shape,) * LINE,
        grid_spec=pltpu.PrefetchScalarGridSpec(
            num_scalar_prefetch=1,
            grid=(LINE // chips,),
            in_specs=in_specs,
            out_specs=(
                pl.BlockSpec((samples, 1, NZ, HALF), lambda i, place: (0, k, 0, 0)),
            )
            * LINE,
            scratch_shapes=[pltpu.VMEM((chips * samples * NZ, HALF), jnp.float32)],
        ),
        input_output_aliases=aliases,
        compiler_params=pltpu.CompilerParams(vmem_limit_bytes=48 << 20),
        cost_estimate=pl.CostEstimate(
            flops=15 * 10**8, transcendentals=0, bytes_accessed=4 << 20
        ),
        name=f"pool_{k}",
    )(place, *operands)


def pair_kernel(place_ref, cot_ref, *rest):
    pooled, outs, (wide_ref, total_ref) = rest[:4], rest[4:8], rest[8:]
    core, ring, line = place_ref[0], place_ref[1], place_ref[2]
    samples = cot_ref.shape[0]

    def spot_of(d, k):
        line_at = (line - d + 4) & 3
        ring_at = (ring + k) & 3
        return jnp.where(core == 0, ring_at * 4 + line_at, line_at * 4 + ring_at)

    for d in range(LINE):
        for k in range(4):
            wide_ref[spot_of(d, k)] = pooled[d][:, k].astype(jnp.float32)
    for s in range(samples):
        wide = wide_ref[:, s].reshape(128, HALF)
        narrow = wide.astype(jnp.bfloat16)
        cot = cot_ref[s]
        total = jnp.dot(cot, narrow, preferred_element_type=jnp.float32)
        total = total + lax.dot_general(
            cot, narrow, (((0,), (0,)), ((), ())), preferred_element_type=jnp.float32
        )
        total = total + POOL_DECAY * wide
        total_ref[:, s] = total.reshape(16, NZ, HALF)
    for d in range(LINE):
        for k in range(4):
            outs[d][:, k] = total_ref[spot_of(d, k)].astype(jnp.bfloat16)


def pair_rows(place, cotangent, pooled):
    samples = cotangent.shape[0]
    step = 32
    spec = pl.BlockSpec((step, 4, NZ, HALF), lambda i, place: (i, 0, 0, 0))
    return pl.pallas_call(
        pair_kernel,
        out_shape=(jax.ShapeDtypeStruct(pooled[0].shape, jnp.bfloat16),) * LINE,
        grid_spec=pltpu.PrefetchScalarGridSpec(
            num_scalar_prefetch=1,
            grid=(samples // step,),
            in_specs=[pl.BlockSpec((step, 128, 128), lambda i, place: (i, 0, 0))] + [spec] * LINE,
            out_specs=(spec,) * LINE,
            scratch_shapes=[pltpu.VMEM((16, step, NZ, HALF), jnp.float32)] * 2,
        ),
        compiler_params=pltpu.CompilerParams(vmem_limit_bytes=48 << 20),
        cost_estimate=pl.CostEstimate(
            flops=4 * samples * 128 * 128 * 256, transcendentals=0, bytes_accessed=12 << 20
        ),
        name="pairwise",
    )(place, cotangent, *pooled)


def spread_kernel(place_ref, idx_low, idx_high, *rest):
    grads_refs = rest[:LINE]
    added = len(rest) == LINE + 5
    before_low, before_high = rest[LINE : LINE + 2] if added else (None, None)
    out_low, out_high, buffer = rest[-3:]
    rows = buffer.shape[0] // NZ
    part = buffer.shape[0] // LINE
    step = pl.program_id(0)
    depth = place_ref[3]

    @pl.when(step == 0)
    def _():
        for d in range(LINE):
            buffer[d * part : (d + 1) * part] = (
                grads_refs[d][...].reshape(part, HALF).astype(jnp.float32)
            )

    iota = lax.broadcasted_iota(jnp.int16, (SLAB, rows), 0)
    for idx_ref, before, out, shift in (
        (idx_low, before_low, out_low, 0),
        (idx_high, before_high, out_high, NZ // 2),
    ):
        at = (depth + step + shift) & 7
        grads = buffer[pl.ds(at, rows, stride=NZ), :].astype(jnp.bfloat16)
        hits = counts_of([idx_ref[0, j : j + 1, :] for j in range(BAG)], iota)
        total = jnp.dot(hits, grads, preferred_element_type=jnp.float32)
        if added:
            total = total + before[0]
        out[0] = total


def spread_rows(k, place, idx, grads, previous):
    samples = grads[0].shape[0]
    rows = LINE * samples
    half = NZ // 2
    operands = [idx, idx, *grads]
    in_specs = [
        pl.BlockSpec((1, BAG, rows), lambda i, place: (k * NZ + i, 0, 0)),
        pl.BlockSpec((1, BAG, rows), lambda i, place: (k * NZ + half + i, 0, 0)),
    ] + [pl.BlockSpec((samples, 1, NZ, HALF), lambda i, place: (0, k, 0, 0))] * LINE
    out_spec = pl.BlockSpec((1, SLAB, HALF), lambda i, place: (i, 0, 0))
    aliases = {}
    if previous is not None:
        operands += list(previous)
        in_specs += [out_spec, out_spec]
        aliases = {7: 0, 8: 1}
    shape = jax.ShapeDtypeStruct((half, SLAB, HALF), jnp.float32)
    return pl.pallas_call(
        spread_kernel,
        out_shape=(shape, shape),
        grid_spec=pltpu.PrefetchScalarGridSpec(
            num_scalar_prefetch=1,
            grid=(half,),
            in_specs=in_specs,
            out_specs=(out_spec, out_spec),
            scratch_shapes=[pltpu.VMEM((rows * NZ, HALF), jnp.float32)],
        ),
        input_output_aliases=aliases,
        compiler_params=pltpu.CompilerParams(vmem_limit_bytes=48 << 20),
        cost_estimate=pl.CostEstimate(
            flops=2 * rows * NZ * SLAB * 256, transcendentals=0, bytes_accessed=6 << 20
        ),
        name=f"spread_{k}",
    )(place, *operands)


def dither_round(weights, dither_bits):
    magnitude = jnp.maximum(jnp.abs(weights), SMALLEST)
    spacing = jnp.exp2(jnp.floor(jnp.log2(magnitude)) - 7.0)
    grid_level = jnp.floor(weights / spacing + dither_bits.astype(jnp.float32) * DITHER_UNIT)
    return (grid_level * spacing).astype(jnp.bfloat16)


def adagrad_rows(slab_rows, grad_rows, state_rows, dither_bits):
    state_next = state_rows + jnp.mean(grad_rows * grad_rows, axis=-1)
    moved = (
        slab_rows.astype(jnp.float32)
        - LEARN_RATE * grad_rows / (jnp.sqrt(state_next) + 1e-08)[:, None]
    )
    return (dither_round(moved, dither_bits), state_next)


def per_device(
    lookup_block, lookup_offset, interaction_grad, table, adagrad_state, touched_blocks, dither
):
    core = lax.axis_index("rep")
    y = lax.axis_index("y")
    x = lax.axis_index("x")
    depth = lax.axis_index("z")
    ring = jnp.where(core == 0, y, x)
    line = jnp.where(core == 0, x, y)
    place = jnp.stack([core, ring, line, depth]).astype(jnp.int32)
    row_count, emb_width = table.shape
    micro_count, sample_count = lookup_block.shape[:2]
    samples = micro_count * sample_count
    touch_count = touched_blocks.shape[1]

    table_blocks = table.reshape(row_count // BLOCK, BLOCK, emb_width)
    slab_table = table_blocks[touched_blocks[0]].reshape(SLAB, emb_width)
    own_half = lax.dynamic_slice(slab_table, (0, core * HALF), (SLAB, HALF))
    near = {i: deep_send(own_half, -i) for i in (1, 2)}
    near.update({8 - i: deep_send(own_half, i) for i in (1, 2)})

    def flat(v):
        return v.transpose(0, 1, 3, 2).reshape(samples, 512).astype(jnp.bfloat16)

    own_lookups = jnp.concatenate([flat(lookup_block), flat(lookup_offset)], axis=1)
    other_lookups, near = lax.optimization_barrier((swap_cores(own_lookups), near))
    both = jnp.concatenate([own_lookups, other_lookups], axis=0)
    other_cot = swap_cores(interaction_grad)
    lane = lax.broadcasted_iota(jnp.int32, (512, 1), 0)
    bag_at = lane // 128
    y_at, x_at, z_at = (lane // 32) % 4, (lane // 8) % 4, (lane - depth + 8) % 8
    line_at = (jnp.where(core == 0, x_at, y_at) - line + 4) % 4
    ring_at = (jnp.where(core == 0, y_at, x_at) - ring + 4) % 4
    goes_to = line_at * 128 + ring_at * 32 + z_at * BAG + bag_at
    moves = goes_to == lax.broadcasted_iota(jnp.int32, (512, 512), 1)
    moves = jnp.concatenate([jnp.where(moves, 64.0, 0.0), jnp.where(moves, 1.0, 0.0)], axis=0)
    rows_out = jnp.dot(both, moves.astype(jnp.bfloat16), preferred_element_type=jnp.float32)
    rows_in = jnp.stack(
        [rows_out[:, :128]]
        + [line_send(rows_out[:, 128 * (LINE - d) : 128 * (LINE - d + 1)], -d) for d in (1, 2, 3)]
    )
    by_sample = [rows_in[:, c * samples : (c + 1) * samples].astype(jnp.int16) for c in range(2)]
    by_lookup = [
        rows_in[:, c * samples : (c + 1) * samples]
        .reshape(LINE * samples, 128)
        .T.astype(jnp.int16)
        .reshape(32, BAG, LINE * samples)
        for c in range(2)
    ]

    middle = SLAB // 2
    opposite = jnp.concatenate(
        [deep_send(near[6][:middle], 2), deep_send(near[2][middle:], -2)], axis=0
    )
    own_slabs = jnp.stack(
        [
            own_half,
            near[1],
            near[2],
            deep_send(near[2], -1),
            opposite,
            deep_send(near[6], 1),
            near[6],
            near[7],
        ]
    )
    own_slabs, by_sample = lax.optimization_barrier((own_slabs, by_sample))
    from_left = ring_send(own_slabs, 1)
    from_right = ring_send(own_slabs, -1)
    pooled = [pool_rows(0, place, by_sample[c], own_slabs, None) for c in range(2)]
    from_left, from_right, pooled = lax.optimization_barrier((from_left, from_right, pooled))
    across = jnp.concatenate(
        [ring_send(from_left[:4], 1), ring_send(from_right[4:], -1)], axis=0
    )
    slabs = {1: from_right, 2: across, 3: from_left}
    for c in range(2):
        if c:
            pooled[1], _ = lax.optimization_barrier((pooled[1], pooled[0]))
        for k in (3, 1, 2):
            pooled[c] = pool_rows(k, place, by_sample[c], slabs[k], pooled[c])

    cots = [
        interaction_grad.reshape(samples, 128, 128),
        other_cot.reshape(samples, 128, 128),
    ]
    grads, paired = [], []
    for c in range(2):
        arrived = [pooled[c][0]] + [line_send(pooled[c][d], d) for d in (1, 2, 3)]
        paired.append(pair_rows(place, cots[c], arrived))
        grads.append([paired[c][0]] + [line_send(paired[c][d], -d) for d in (1, 2, 3)])
    early, _ = lax.optimization_barrier((grads[0], paired[1]))
    partial = {}
    for k in (2, 1, 3, 0):
        partial[k] = spread_rows(k, place, by_lookup[0], early, None)
    late, partial = lax.optimization_barrier((grads[1], partial))
    for k in (2, 1, 3, 0):
        partial[k] = spread_rows(k, place, by_lookup[1], late, partial[k])

    low_one = ring_send(partial[1][0] + ring_send(partial[2][0], 1), 1)
    high_three = ring_send(partial[3][1] + ring_send(partial[2][1], -1), -1)
    high_one = ring_send(partial[1][1], 1)
    low_three = ring_send(partial[3][0], -1)
    low = partial[0][0] + low_one + low_three
    high = partial[0][1] + high_one + high_three
    up = low[3] + jnp.pad(deep_send(high[0, :middle], 1), ((0, middle), (0, 0)))
    down = high[1] + jnp.pad(deep_send(high[0, middle:], -1), ((middle, 0), (0, 0)))
    for i in (2, 1, 0):
        up = deep_send(up, 1)
        down = deep_send(down, -1)
        if i:
            up = low[i] + up
            down = high[4 - i] + down
    own_grad = low[0] + up + down
    other_grad = swap_cores(own_grad)
    summed_grad = jnp.where(
        core == 0,
        jnp.concatenate([own_grad, other_grad], axis=1),
        jnp.concatenate([other_grad, own_grad], axis=1),
    )

    state_blocks = adagrad_state.reshape(row_count // BLOCK, BLOCK)
    state_slab = state_blocks[touched_blocks[0]].reshape(SLAB)
    new_rows, state_next = adagrad_rows(slab_table, summed_grad, state_slab, dither[0])
    updated_blocks = table_blocks.at[touched_blocks[0]].set(
        new_rows.reshape(touch_count, BLOCK, emb_width)
    )
    updated_state = state_blocks.at[touched_blocks[0]].set(state_next.reshape(touch_count, BLOCK))
    return (updated_blocks.reshape(row_count, emb_width), updated_state.reshape(row_count))


def solution(mesh):
    fine = Mesh(mesh.devices.reshape(2, NY, NX, NZ), AXES)
    tables = ("y", "x", "z")
    return jax.shard_map(
        per_device,
        mesh=fine,
        in_specs=(
            P(None, AXES, None, None),
            P(None, AXES, None, None),
            P(None, AXES, None, None),
            P(tables, None),
            P(tables),
            P(tables, None),
            P(tables, None, None),
        ),
        out_specs=(P(tables, None), P(tables)),
        check_vma=False,
    )
```

```python
import jax
import jax.numpy as jnp
from jax import lax
from jax.experimental import pallas as pl
from jax.experimental.pallas import tpu as pltpu
from jax.sharding import Mesh
from jax.sharding import PartitionSpec as P

BLOCK = 64
LEARN_RATE = 0.1
POOL_DECAY = 0.5
DITHER_UNIT = 2.0 ** (-15)
SMALLEST = 2.0 ** (-14)

NY, NX, NZ = 4, 4, 8
LINE = 4
HALF = 128
SLAB = 640
BAG = 4
AXES = ("rep", "y", "x", "z")


def device_id(r, y, x, z):
    return ((r * NY + y) * NX + x) * NZ + z


def moves_along(step_first, step_second):
    pairs = []
    for y in range(NY):
        for x in range(NX):
            for z in range(NZ):
                for core, (dy, dx, dz) in enumerate((step_first, step_second)):
                    to = device_id(core, (y + dy) % NY, (x + dx) % NX, (z + dz) % NZ)
                    pairs.append((device_id(core, y, x, z), to))
    return pairs


def ring_send(value, step):
    return lax.ppermute(value, AXES, moves_along((step, 0, 0), (0, step, 0)))


def line_send(value, step):
    return lax.ppermute(value, AXES, moves_along((0, step, 0), (step, 0, 0)))


def deep_send(value, step):
    return lax.ppermute(value, AXES, moves_along((0, 0, step), (0, 0, step)))


def swap_cores(value):
    return lax.ppermute(value, "rep", [(0, 1), (1, 0)])


def counts_of(columns, iota):
    one = jnp.ones((), jnp.bfloat16)
    zero = jnp.zeros((), jnp.bfloat16)
    total = None
    for column in columns:
        hit = jnp.where(column == iota, one, zero)
        total = hit if total is None else total + hit
    return total


def pool_kernel(k, place_ref, idx_ref, slab_ref, *rest):
    outs, buffer = rest[-LINE - 1 : -1], rest[-1]
    depth = place_ref[3]
    step = pl.program_id(0)
    chips, samples = idx_ref.shape[:2]
    rows = chips * samples
    idx = idx_ref[...].reshape(rows, 128)
    iota = lax.broadcasted_iota(jnp.int16, (rows, SLAB), 1)
    for i in range(NZ):
        base = k * 32 + i * BAG
        hits = counts_of([idx[:, base + j : base + j + 1] for j in range(BAG)], iota)
        rows_sum = jnp.dot(hits, slab_ref[i], preferred_element_type=jnp.float32)
        buffer[pl.ds((depth + i) & 7, rows, stride=NZ), :] = rows_sum
    for d in range(LINE):
        first = (d % chips) * samples * NZ

        @pl.when(step == d // chips)
        def _():
            outs[d][...] = (
                buffer[first : first + samples * NZ]
                .astype(jnp.bfloat16)
                .reshape(samples, 1, NZ, HALF)
            )


def pool_rows(k, place, idx, slabs, previous):
    samples = idx.shape[1]
    chips = 2
    operands = [idx, slabs]
    in_specs = [
        pl.BlockSpec((chips, samples, 128), lambda i, place: (i, 0, 0)),
        pl.BlockSpec((NZ, SLAB, HALF), lambda i, place: (0, 0, 0)),
    ]
    aliases = {}
    if previous is not None:
        operands += list(previous)
        in_specs += [pl.BlockSpec(memory_space=pl.ANY)] * LINE
        aliases = {3 + d: d for d in range(LINE)}
    shape = jax.ShapeDtypeStruct((samples, 4, NZ, HALF), jnp.bfloat16)
    return pl.pallas_call(
        lambda *refs: pool_kernel(k, *refs),
        out_shape=(shape,) * LINE,
        grid_spec=pltpu.PrefetchScalarGridSpec(
            num_scalar_prefetch=1,
            grid=(LINE // chips,),
            in_specs=in_specs,
            out_specs=(
                pl.BlockSpec((samples, 1, NZ, HALF), lambda i, place: (0, k, 0, 0)),
            )
            * LINE,
            scratch_shapes=[pltpu.VMEM((chips * samples * NZ, HALF), jnp.float32)],
        ),
        input_output_aliases=aliases,
        compiler_params=pltpu.CompilerParams(vmem_limit_bytes=48 << 20),
        cost_estimate=pl.CostEstimate(
            flops=15 * 10**8, transcendentals=0, bytes_accessed=4 << 20
        ),
        name=f"pool_{k}",
    )(place, *operands)


def pair_kernel(place_ref, cot_ref, *rest):
    pooled, outs, (wide_ref, total_ref) = rest[:4], rest[4:8], rest[8:]
    core, ring, line = place_ref[0], place_ref[1], place_ref[2]
    samples = cot_ref.shape[0]

    def spot_of(d, k):
        line_at = (line - d + 4) & 3
        ring_at = (ring + k) & 3
        return jnp.where(core == 0, ring_at * 4 + line_at, line_at * 4 + ring_at)

    for d in range(LINE):
        for k in range(4):
            wide_ref[spot_of(d, k)] = pooled[d][:, k].astype(jnp.float32)
    for s in range(samples):
        wide = wide_ref[:, s].reshape(128, HALF)
        narrow = wide.astype(jnp.bfloat16)
        cot = cot_ref[s]
        total = jnp.dot(cot, narrow, preferred_element_type=jnp.float32)
        total = total + lax.dot_general(
            cot, narrow, (((0,), (0,)), ((), ())), preferred_element_type=jnp.float32
        )
        total = total + POOL_DECAY * wide
        total_ref[:, s] = total.reshape(16, NZ, HALF)
    for d in range(LINE):
        for k in range(4):
            outs[d][:, k] = total_ref[spot_of(d, k)].astype(jnp.bfloat16)


def pair_rows(place, cotangent, pooled):
    samples = cotangent.shape[0]
    step = 32
    spec = pl.BlockSpec((step, 4, NZ, HALF), lambda i, place: (i, 0, 0, 0))
    return pl.pallas_call(
        pair_kernel,
        out_shape=(jax.ShapeDtypeStruct(pooled[0].shape, jnp.bfloat16),) * LINE,
        grid_spec=pltpu.PrefetchScalarGridSpec(
            num_scalar_prefetch=1,
            grid=(samples // step,),
            in_specs=[pl.BlockSpec((step, 128, 128), lambda i, place: (i, 0, 0))] + [spec] * LINE,
            out_specs=(spec,) * LINE,
            scratch_shapes=[pltpu.VMEM((16, step, NZ, HALF), jnp.float32)] * 2,
        ),
        compiler_params=pltpu.CompilerParams(vmem_limit_bytes=48 << 20),
        cost_estimate=pl.CostEstimate(
            flops=4 * samples * 128 * 128 * 256, transcendentals=0, bytes_accessed=12 << 20
        ),
        name="pairwise",
    )(place, cotangent, *pooled)


def spread_kernel(place_ref, idx_low, idx_high, *rest):
    grads_refs = rest[:LINE]
    added = len(rest) == LINE + 5
    before_low, before_high = rest[LINE : LINE + 2] if added else (None, None)
    out_low, out_high, buffer = rest[-3:]
    rows = buffer.shape[0] // NZ
    part = buffer.shape[0] // LINE
    step = pl.program_id(0)
    depth = place_ref[3]

    @pl.when(step == 0)
    def _():
        for d in range(LINE):
            buffer[d * part : (d + 1) * part] = (
                grads_refs[d][...].reshape(part, HALF).astype(jnp.float32)
            )

    iota = lax.broadcasted_iota(jnp.int16, (SLAB, rows), 0)
    for idx_ref, before, out, shift in (
        (idx_low, before_low, out_low, 0),
        (idx_high, before_high, out_high, NZ // 2),
    ):
        at = (depth + step + shift) & 7
        grads = buffer[pl.ds(at, rows, stride=NZ), :].astype(jnp.bfloat16)
        hits = counts_of([idx_ref[0, j : j + 1, :] for j in range(BAG)], iota)
        total = jnp.dot(hits, grads, preferred_element_type=jnp.float32)
        if added:
            total = total + before[0]
        out[0] = total


def spread_rows(k, place, idx, grads, previous):
    samples = grads[0].shape[0]
    rows = LINE * samples
    half = NZ // 2
    operands = [idx, idx, *grads]
    in_specs = [
        pl.BlockSpec((1, BAG, rows), lambda i, place: (k * NZ + i, 0, 0)),
        pl.BlockSpec((1, BAG, rows), lambda i, place: (k * NZ + half + i, 0, 0)),
    ] + [pl.BlockSpec((samples, 1, NZ, HALF), lambda i, place: (0, k, 0, 0))] * LINE
    out_spec = pl.BlockSpec((1, SLAB, HALF), lambda i, place: (i, 0, 0))
    aliases = {}
    if previous is not None:
        operands += list(previous)
        in_specs += [out_spec, out_spec]
        aliases = {7: 0, 8: 1}
    shape = jax.ShapeDtypeStruct((half, SLAB, HALF), jnp.float32)
    return pl.pallas_call(
        spread_kernel,
        out_shape=(shape, shape),
        grid_spec=pltpu.PrefetchScalarGridSpec(
            num_scalar_prefetch=1,
            grid=(half,),
            in_specs=in_specs,
            out_specs=(out_spec, out_spec),
            scratch_shapes=[pltpu.VMEM((rows * NZ, HALF), jnp.float32)],
        ),
        input_output_aliases=aliases,
        compiler_params=pltpu.CompilerParams(vmem_limit_bytes=48 << 20),
        cost_estimate=pl.CostEstimate(
            flops=2 * rows * NZ * SLAB * 256, transcendentals=0, bytes_accessed=6 << 20
        ),
        name=f"spread_{k}",
    )(place, *operands)


def dither_round(weights, dither_bits):
    magnitude = jnp.maximum(jnp.abs(weights), SMALLEST)
    spacing = jnp.exp2(jnp.floor(jnp.log2(magnitude)) - 7.0)
    grid_level = jnp.floor(weights / spacing + dither_bits.astype(jnp.float32) * DITHER_UNIT)
    return (grid_level * spacing).astype(jnp.bfloat16)


def adagrad_rows(slab_rows, grad_rows, state_rows, dither_bits):
    state_next = state_rows + jnp.mean(grad_rows * grad_rows, axis=-1)
    moved = (
        slab_rows.astype(jnp.float32)
        - LEARN_RATE * grad_rows / (jnp.sqrt(state_next) + 1e-08)[:, None]
    )
    return (dither_round(moved, dither_bits), state_next)


def per_device(
    lookup_block, lookup_offset, interaction_grad, table, adagrad_state, touched_blocks, dither
):
    core = lax.axis_index("rep")
    y = lax.axis_index("y")
    x = lax.axis_index("x")
    depth = lax.axis_index("z")
    ring = jnp.where(core == 0, y, x)
    line = jnp.where(core == 0, x, y)
    place = jnp.stack([core, ring, line, depth]).astype(jnp.int32)
    row_count, emb_width = table.shape
    micro_count, sample_count = lookup_block.shape[:2]
    samples = micro_count * sample_count
    touch_count = touched_blocks.shape[1]

    table_blocks = table.reshape(row_count // BLOCK, BLOCK, emb_width)
    slab_table = table_blocks[touched_blocks[0]].reshape(SLAB, emb_width)
    own_half = lax.dynamic_slice(slab_table, (0, core * HALF), (SLAB, HALF))
    near = {2: deep_send(own_half, -2), 6: deep_send(own_half, 2)}

    def flat(v):
        return v.transpose(0, 1, 3, 2).reshape(samples, 512).astype(jnp.bfloat16)

    own_lookups = jnp.concatenate([flat(lookup_block), flat(lookup_offset)], axis=1)
    other_lookups, near = lax.optimization_barrier((swap_cores(own_lookups), near))
    both = jnp.concatenate([own_lookups, other_lookups], axis=0)
    lane = lax.broadcasted_iota(jnp.int32, (512, 1), 0)
    bag_at = lane // 128
    y_at, x_at, z_at = (lane // 32) % 4, (lane // 8) % 4, (lane - depth + 8) % 8
    line_at = (jnp.where(core == 0, x_at, y_at) - line + 4) % 4
    ring_at = (jnp.where(core == 0, y_at, x_at) - ring + 4) % 4
    goes_to = line_at * 128 + ring_at * 32 + z_at * BAG + bag_at
    moves = goes_to == lax.broadcasted_iota(jnp.int32, (512, 512), 1)
    moves = jnp.concatenate([jnp.where(moves, 64.0, 0.0), jnp.where(moves, 1.0, 0.0)], axis=0)
    rows_out = jnp.dot(both, moves.astype(jnp.bfloat16), preferred_element_type=jnp.float32)
    rows_in = jnp.stack(
        [rows_out[:, :128]]
        + [line_send(rows_out[:, 128 * (LINE - d) : 128 * (LINE - d + 1)], -d) for d in (1, 2, 3)]
    )
    by_sample = [rows_in[:, c * samples : (c + 1) * samples].astype(jnp.int16) for c in range(2)]
    by_lookup = [
        rows_in[:, c * samples : (c + 1) * samples]
        .reshape(LINE * samples, 128)
        .T.astype(jnp.int16)
        .reshape(32, BAG, LINE * samples)
        for c in range(2)
    ]

    middle = SLAB // 2
    opposite = jnp.concatenate(
        [deep_send(near[6][:middle], 2), deep_send(near[2][middle:], -2)], axis=0
    )
    again, _ = lax.optimization_barrier((own_half, near))
    near[1], near[7] = deep_send(again, -1), deep_send(again, 1)
    own_slabs = jnp.stack(
        [
            own_half,
            near[1],
            near[2],
            deep_send(near[2], -1),
            opposite,
            deep_send(near[6], 1),
            near[6],
            near[7],
        ]
    )
    own_slabs, by_sample = lax.optimization_barrier((own_slabs, by_sample))
    from_left = ring_send(own_slabs, 1)
    from_right = ring_send(own_slabs, -1)
    pooled = [pool_rows(0, place, by_sample[c], own_slabs, None) for c in range(2)]
    from_left, from_right, pooled = lax.optimization_barrier((from_left, from_right, pooled))
    across = jnp.concatenate(
        [ring_send(from_left[:4], 1), ring_send(from_right[4:], -1)], axis=0
    )
    slabs = {1: from_right, 2: across, 3: from_left}
    for c in range(2):
        if c:
            pooled[1], own_cot, _ = lax.optimization_barrier(
                (pooled[1], interaction_grad, pooled[0])
            )
            other_cot = swap_cores(own_cot)
        for k in (3, 1, 2):
            pooled[c] = pool_rows(k, place, by_sample[c], slabs[k], pooled[c])

    cots = [
        interaction_grad.reshape(samples, 128, 128),
        other_cot.reshape(samples, 128, 128),
    ]
    grads, paired = [], []
    for c in range(2):
        arrived = [pooled[c][0]] + [line_send(pooled[c][d], d) for d in (1, 2, 3)]
        paired.append(pair_rows(place, cots[c], arrived))
        grads.append([paired[c][0]] + [line_send(paired[c][d], -d) for d in (1, 2, 3)])
    early, _ = lax.optimization_barrier((grads[0], paired[1]))
    partial = {}
    for k in (2, 1, 3, 0):
        partial[k] = spread_rows(k, place, by_lookup[0], early, None)
    late, partial = lax.optimization_barrier((grads[1], partial))
    for k in (2, 3, 1, 0):
        partial[k] = spread_rows(k, place, by_lookup[1], late, partial[k])
        late, _ = lax.optimization_barrier((late, partial[k]))
    low = {k: partial[k][0] for k in partial}
    high = {k: partial[k][1] for k in partial}

    high_three = ring_send(high[3] + ring_send(high[2], -1), -1)
    high_one = ring_send(high[1], 1)
    low_one = ring_send(low[1] + ring_send(low[2], 1), 1)
    low_three = ring_send(low[3], -1)
    high = high[0] + high_one + high_three
    low = low[0] + low_one + low_three
    from_behind, from_ahead = deep_send(low[3], 1), deep_send(high[1], -1)
    upper, lower = deep_send(high[0, :middle], 2), deep_send(high[0, middle:], -2)
    up = low[2] + from_behind + jnp.pad(upper, ((0, middle), (0, 0)))
    down = high[2] + from_ahead + jnp.pad(lower, ((middle, 0), (0, 0)))
    own_grad = (
        low[0]
        + deep_send(low[1], 1)
        + deep_send(high[3], -1)
        + deep_send(up, 2)
        + deep_send(down, -2)
    )
    other_grad = swap_cores(own_grad)
    summed_grad = jnp.where(
        core == 0,
        jnp.concatenate([own_grad, other_grad], axis=1),
        jnp.concatenate([other_grad, own_grad], axis=1),
    )

    state_blocks = adagrad_state.reshape(row_count // BLOCK, BLOCK)
    state_slab = state_blocks[touched_blocks[0]].reshape(SLAB)
    new_rows, state_next = adagrad_rows(slab_table, summed_grad, state_slab, dither[0])
    updated_blocks = table_blocks.at[touched_blocks[0]].set(
        new_rows.reshape(touch_count, BLOCK, emb_width)
    )
    updated_state = state_blocks.at[touched_blocks[0]].set(state_next.reshape(touch_count, BLOCK))
    return (updated_blocks.reshape(row_count, emb_width), updated_state.reshape(row_count))


def solution(mesh):
    fine = Mesh(mesh.devices.reshape(2, NY, NX, NZ), AXES)
    tables = ("y", "x", "z")
    return jax.shard_map(
        per_device,
        mesh=fine,
        in_specs=(
            P(None, AXES, None, None),
            P(None, AXES, None, None),
            P(None, AXES, None, None),
            P(tables, None),
            P(tables),
            P(tables, None),
            P(tables, None, None),
        ),
        out_specs=(P(tables, None), P(tables)),
        check_vma=False,
    )
```

```python
import jax
import jax.numpy as jnp
from jax import lax
from jax.experimental import pallas as pl
from jax.experimental.pallas import tpu as pltpu
from jax.sharding import Mesh
from jax.sharding import PartitionSpec as P

BLOCK = 64
LEARN_RATE = 0.1
POOL_DECAY = 0.5
DITHER_UNIT = 2.0 ** (-15)
SMALLEST = 2.0 ** (-14)

NY, NX, NZ = 4, 4, 8
LINE = 4
HALF = 128
SLAB = 640
BAG = 4
AXES = ("rep", "y", "x", "z")


def device_id(r, y, x, z):
    return ((r * NY + y) * NX + x) * NZ + z


def moves_along(step_first, step_second):
    pairs = []
    for y in range(NY):
        for x in range(NX):
            for z in range(NZ):
                for core, (dy, dx, dz) in enumerate((step_first, step_second)):
                    to = device_id(core, (y + dy) % NY, (x + dx) % NX, (z + dz) % NZ)
                    pairs.append((device_id(core, y, x, z), to))
    return pairs


def ring_send(value, step):
    return lax.ppermute(value, AXES, moves_along((step, 0, 0), (0, step, 0)))


def line_send(value, step):
    return lax.ppermute(value, AXES, moves_along((0, step, 0), (step, 0, 0)))


def deep_send(value, step):
    return lax.ppermute(value, AXES, moves_along((0, 0, step), (0, 0, step)))


def swap_cores(value):
    return lax.ppermute(value, "rep", [(0, 1), (1, 0)])


def counts_of(columns, iota):
    one = jnp.ones((), jnp.bfloat16)
    zero = jnp.zeros((), jnp.bfloat16)
    total = None
    for column in columns:
        hit = jnp.where(column == iota, one, zero)
        total = hit if total is None else total + hit
    return total


def pool_kernel(k, place_ref, idx_ref, slab_ref, *rest):
    outs, buffer = rest[-LINE - 1 : -1], rest[-1]
    depth = place_ref[3]
    step = pl.program_id(0)
    chips, samples = idx_ref.shape[:2]
    rows = chips * samples
    idx = idx_ref[...].reshape(rows, 128)
    iota = lax.broadcasted_iota(jnp.int16, (rows, SLAB), 1)
    for i in range(NZ):
        base = k * 32 + i * BAG
        hits = counts_of([idx[:, base + j : base + j + 1] for j in range(BAG)], iota)
        rows_sum = jnp.dot(hits, slab_ref[i], preferred_element_type=jnp.float32)
        buffer[pl.ds((depth + i) & 7, rows, stride=NZ), :] = rows_sum
    for d in range(LINE):
        first = (d % chips) * samples * NZ

        @pl.when(step == d // chips)
        def _():
            outs[d][...] = (
                buffer[first : first + samples * NZ]
                .astype(jnp.bfloat16)
                .reshape(samples, 1, NZ, HALF)
            )


def pool_rows(k, place, idx, slabs, previous):
    samples = idx.shape[1]
    chips = 2
    operands = [idx, slabs]
    in_specs = [
        pl.BlockSpec((chips, samples, 128), lambda i, place: (i, 0, 0)),
        pl.BlockSpec((NZ, SLAB, HALF), lambda i, place: (0, 0, 0)),
    ]
    aliases = {}
    if previous is not None:
        operands += list(previous)
        in_specs += [pl.BlockSpec(memory_space=pl.ANY)] * LINE
        aliases = {3 + d: d for d in range(LINE)}
    shape = jax.ShapeDtypeStruct((samples, 4, NZ, HALF), jnp.bfloat16)
    return pl.pallas_call(
        lambda *refs: pool_kernel(k, *refs),
        out_shape=(shape,) * LINE,
        grid_spec=pltpu.PrefetchScalarGridSpec(
            num_scalar_prefetch=1,
            grid=(LINE // chips,),
            in_specs=in_specs,
            out_specs=(
                pl.BlockSpec((samples, 1, NZ, HALF), lambda i, place: (0, k, 0, 0)),
            )
            * LINE,
            scratch_shapes=[pltpu.VMEM((chips * samples * NZ, HALF), jnp.float32)],
        ),
        input_output_aliases=aliases,
        compiler_params=pltpu.CompilerParams(vmem_limit_bytes=48 << 20),
        cost_estimate=pl.CostEstimate(
            flops=15 * 10**8, transcendentals=0, bytes_accessed=4 << 20
        ),
        name=f"pool_{k}",
    )(place, *operands)


def pair_kernel(place_ref, cot_ref, *rest):
    pooled, outs, (wide_ref, total_ref) = rest[:4], rest[4:8], rest[8:]
    core, ring, line = place_ref[0], place_ref[1], place_ref[2]
    samples = cot_ref.shape[0]

    def spot_of(d, k):
        line_at = (line - d + 4) & 3
        ring_at = (ring + k) & 3
        return jnp.where(core == 0, ring_at * 4 + line_at, line_at * 4 + ring_at)

    for d in range(LINE):
        for k in range(4):
            wide_ref[spot_of(d, k)] = pooled[d][:, k].astype(jnp.float32)
    for s in range(samples):
        wide = wide_ref[:, s].reshape(128, HALF)
        narrow = wide.astype(jnp.bfloat16)
        cot = cot_ref[s]
        total = jnp.dot(cot, narrow, preferred_element_type=jnp.float32)
        total = total + lax.dot_general(
            cot, narrow, (((0,), (0,)), ((), ())), preferred_element_type=jnp.float32
        )
        total = total + POOL_DECAY * wide
        total_ref[:, s] = total.reshape(16, NZ, HALF)
    for d in range(LINE):
        for k in range(4):
            outs[d][:, k] = total_ref[spot_of(d, k)].astype(jnp.bfloat16)


def pair_rows(place, cotangent, pooled):
    samples = cotangent.shape[0]
    step = 32
    spec = pl.BlockSpec((step, 4, NZ, HALF), lambda i, place: (i, 0, 0, 0))
    return pl.pallas_call(
        pair_kernel,
        out_shape=(jax.ShapeDtypeStruct(pooled[0].shape, jnp.bfloat16),) * LINE,
        grid_spec=pltpu.PrefetchScalarGridSpec(
            num_scalar_prefetch=1,
            grid=(samples // step,),
            in_specs=[pl.BlockSpec((step, 128, 128), lambda i, place: (i, 0, 0))] + [spec] * LINE,
            out_specs=(spec,) * LINE,
            scratch_shapes=[pltpu.VMEM((16, step, NZ, HALF), jnp.float32)] * 2,
        ),
        compiler_params=pltpu.CompilerParams(vmem_limit_bytes=48 << 20),
        cost_estimate=pl.CostEstimate(
            flops=4 * samples * 128 * 128 * 256, transcendentals=0, bytes_accessed=12 << 20
        ),
        name="pairwise",
    )(place, cotangent, *pooled)


def spread_kernel(place_ref, idx_low, idx_high, *rest):
    grads_refs = rest[:LINE]
    added = len(rest) == LINE + 5
    before_low, before_high = rest[LINE : LINE + 2] if added else (None, None)
    out_low, out_high, buffer = rest[-3:]
    rows = buffer.shape[0] // NZ
    part = buffer.shape[0] // LINE
    step = pl.program_id(0)
    depth = place_ref[3]

    @pl.when(step == 0)
    def _():
        for d in range(LINE):
            buffer[d * part : (d + 1) * part] = (
                grads_refs[d][...].reshape(part, HALF).astype(jnp.float32)
            )

    iota = lax.broadcasted_iota(jnp.int16, (SLAB, rows), 0)
    for idx_ref, before, out, shift in (
        (idx_low, before_low, out_low, 0),
        (idx_high, before_high, out_high, NZ // 2),
    ):
        at = (depth + step + shift) & 7
        grads = buffer[pl.ds(at, rows, stride=NZ), :].astype(jnp.bfloat16)
        hits = counts_of([idx_ref[0, j : j + 1, :] for j in range(BAG)], iota)
        total = jnp.dot(hits, grads, preferred_element_type=jnp.float32)
        if added:
            total = total + before[0]
        out[0] = total


def spread_rows(k, place, idx, grads, previous):
    samples = grads[0].shape[0]
    rows = LINE * samples
    half = NZ // 2
    operands = [idx, idx, *grads]
    in_specs = [
        pl.BlockSpec((1, BAG, rows), lambda i, place: (k * NZ + i, 0, 0)),
        pl.BlockSpec((1, BAG, rows), lambda i, place: (k * NZ + half + i, 0, 0)),
    ] + [pl.BlockSpec((samples, 1, NZ, HALF), lambda i, place: (0, k, 0, 0))] * LINE
    out_spec = pl.BlockSpec((1, SLAB, HALF), lambda i, place: (i, 0, 0))
    aliases = {}
    if previous is not None:
        operands += list(previous)
        in_specs += [out_spec, out_spec]
        aliases = {7: 0, 8: 1}
    shape = jax.ShapeDtypeStruct((half, SLAB, HALF), jnp.float32)
    return pl.pallas_call(
        spread_kernel,
        out_shape=(shape, shape),
        grid_spec=pltpu.PrefetchScalarGridSpec(
            num_scalar_prefetch=1,
            grid=(half,),
            in_specs=in_specs,
            out_specs=(out_spec, out_spec),
            scratch_shapes=[pltpu.VMEM((rows * NZ, HALF), jnp.float32)],
        ),
        input_output_aliases=aliases,
        compiler_params=pltpu.CompilerParams(vmem_limit_bytes=48 << 20),
        cost_estimate=pl.CostEstimate(
            flops=2 * rows * NZ * SLAB * 256, transcendentals=0, bytes_accessed=6 << 20
        ),
        name=f"spread_{k}",
    )(place, *operands)


def dither_round(weights, dither_bits):
    magnitude = jnp.maximum(jnp.abs(weights), SMALLEST)
    spacing = jnp.exp2(jnp.floor(jnp.log2(magnitude)) - 7.0)
    grid_level = jnp.floor(weights / spacing + dither_bits.astype(jnp.float32) * DITHER_UNIT)
    return (grid_level * spacing).astype(jnp.bfloat16)


def adagrad_rows(slab_rows, grad_rows, state_rows, dither_bits):
    state_next = state_rows + jnp.mean(grad_rows * grad_rows, axis=-1)
    moved = (
        slab_rows.astype(jnp.float32)
        - LEARN_RATE * grad_rows / (jnp.sqrt(state_next) + 1e-08)[:, None]
    )
    return (dither_round(moved, dither_bits), state_next)


def per_device(
    lookup_block, lookup_offset, interaction_grad, table, adagrad_state, touched_blocks, dither
):
    core = lax.axis_index("rep")
    y = lax.axis_index("y")
    x = lax.axis_index("x")
    depth = lax.axis_index("z")
    ring = jnp.where(core == 0, y, x)
    line = jnp.where(core == 0, x, y)
    place = jnp.stack([core, ring, line, depth]).astype(jnp.int32)
    row_count, emb_width = table.shape
    micro_count, sample_count = lookup_block.shape[:2]
    samples = micro_count * sample_count
    touch_count = touched_blocks.shape[1]

    table_blocks = table.reshape(row_count // BLOCK, BLOCK, emb_width)
    slab_table = table_blocks[touched_blocks[0]].reshape(SLAB, emb_width)
    own_half = lax.dynamic_slice(slab_table, (0, core * HALF), (SLAB, HALF))
    near = {2: deep_send(own_half, -2), 6: deep_send(own_half, 2)}

    def flat(v):
        return v.transpose(0, 1, 3, 2).reshape(samples, 512).astype(jnp.bfloat16)

    own_lookups = jnp.concatenate([flat(lookup_block), flat(lookup_offset)], axis=1)
    other_lookups, near = lax.optimization_barrier((swap_cores(own_lookups), near))
    both = jnp.concatenate([own_lookups, other_lookups], axis=0)
    lane = lax.broadcasted_iota(jnp.int32, (512, 1), 0)
    bag_at = lane // 128
    y_at, x_at, z_at = (lane // 32) % 4, (lane // 8) % 4, (lane - depth + 8) % 8
    line_at = (jnp.where(core == 0, x_at, y_at) - line + 4) % 4
    ring_at = (jnp.where(core == 0, y_at, x_at) - ring + 4) % 4
    goes_to = line_at * 128 + ring_at * 32 + z_at * BAG + bag_at
    moves = goes_to == lax.broadcasted_iota(jnp.int32, (512, 512), 1)
    moves = jnp.concatenate([jnp.where(moves, 64.0, 0.0), jnp.where(moves, 1.0, 0.0)], axis=0)
    rows_out = jnp.dot(both, moves.astype(jnp.bfloat16), preferred_element_type=jnp.float32)
    rows_in = jnp.stack(
        [rows_out[:, :128]]
        + [line_send(rows_out[:, 128 * (LINE - d) : 128 * (LINE - d + 1)], -d) for d in (1, 2, 3)]
    )
    by_sample = [rows_in[:, c * samples : (c + 1) * samples].astype(jnp.int16) for c in range(2)]
    by_lookup = [
        rows_in[:, c * samples : (c + 1) * samples]
        .reshape(LINE * samples, 128)
        .T.astype(jnp.int16)
        .reshape(32, BAG, LINE * samples)
        for c in range(2)
    ]

    middle = SLAB // 2
    opposite = jnp.concatenate(
        [deep_send(near[6][:middle], 2), deep_send(near[2][middle:], -2)], axis=0
    )
    again, _ = lax.optimization_barrier((own_half, near))
    near[1], near[7] = deep_send(again, -1), deep_send(again, 1)
    own_slabs = jnp.stack(
        [
            own_half,
            near[1],
            near[2],
            deep_send(near[2], -1),
            opposite,
            deep_send(near[6], 1),
            near[6],
            near[7],
        ]
    )
    own_slabs, by_sample = lax.optimization_barrier((own_slabs, by_sample))
    from_left = ring_send(own_slabs, 1)
    from_right = ring_send(own_slabs, -1)
    pooled = [pool_rows(0, place, by_sample[c], own_slabs, None) for c in range(2)]
    from_left, from_right, pooled = lax.optimization_barrier((from_left, from_right, pooled))
    across = jnp.concatenate(
        [ring_send(from_left[:4], 1), ring_send(from_right[4:], -1)], axis=0
    )
    slabs = {1: from_right, 2: across, 3: from_left}
    for c in range(2):
        if c:
            pooled[1], own_cot, _ = lax.optimization_barrier(
                (pooled[1], interaction_grad, pooled[0])
            )
            other_cot = swap_cores(own_cot)
        for k in (3, 1, 2):
            pooled[c] = pool_rows(k, place, by_sample[c], slabs[k], pooled[c])

    cots = [
        interaction_grad.reshape(samples, 128, 128),
        other_cot.reshape(samples, 128, 128),
    ]
    grads, paired = [], []
    for c in range(2):
        arrived = [pooled[c][0]] + [line_send(pooled[c][d], d) for d in (1, 2, 3)]
        paired.append(pair_rows(place, cots[c], arrived))
        grads.append([paired[c][0]] + [line_send(paired[c][d], -d) for d in (1, 2, 3)])
    early, _ = lax.optimization_barrier((grads[0], paired[1]))
    partial = {k: spread_rows(k, place, by_lookup[0], early, None) for k in (2, 1, 3)}
    late, partial = lax.optimization_barrier((grads[1], partial))
    for k in (2, 1, 3):
        partial[k] = spread_rows(k, place, by_lookup[1], late, partial[k])
    early, late, _ = lax.optimization_barrier((early, late, (partial[1], partial[3])))
    partial[0] = spread_rows(0, place, by_lookup[0], early, None)
    partial[0] = spread_rows(0, place, by_lookup[1], late, partial[0])

    low_one = ring_send(partial[1][0] + ring_send(partial[2][0], 1), 1)
    high_three = ring_send(partial[3][1] + ring_send(partial[2][1], -1), -1)
    high_one = ring_send(partial[1][1], 1)
    low_three = ring_send(partial[3][0], -1)
    low = partial[0][0] + low_one + low_three
    high = partial[0][1] + high_one + high_three
    up = low[3] + jnp.pad(deep_send(high[0, :middle], 1), ((0, middle), (0, 0)))
    down = high[1] + jnp.pad(deep_send(high[0, middle:], -1), ((middle, 0), (0, 0)))
    for i in (2, 1, 0):
        up = deep_send(up, 1)
        down = deep_send(down, -1)
        if i:
            up = low[i] + up
            down = high[4 - i] + down
    own_grad = low[0] + up + down
    other_grad = swap_cores(own_grad)
    summed_grad = jnp.where(
        core == 0,
        jnp.concatenate([own_grad, other_grad], axis=1),
        jnp.concatenate([other_grad, own_grad], axis=1),
    )

    state_blocks = adagrad_state.reshape(row_count // BLOCK, BLOCK)
    state_slab = state_blocks[touched_blocks[0]].reshape(SLAB)
    new_rows, state_next = adagrad_rows(slab_table, summed_grad, state_slab, dither[0])
    updated_blocks = table_blocks.at[touched_blocks[0]].set(
        new_rows.reshape(touch_count, BLOCK, emb_width)
    )
    updated_state = state_blocks.at[touched_blocks[0]].set(state_next.reshape(touch_count, BLOCK))
    return (updated_blocks.reshape(row_count, emb_width), updated_state.reshape(row_count))


def solution(mesh):
    fine = Mesh(mesh.devices.reshape(2, NY, NX, NZ), AXES)
    tables = ("y", "x", "z")
    return jax.shard_map(
        per_device,
        mesh=fine,
        in_specs=(
            P(None, AXES, None, None),
            P(None, AXES, None, None),
            P(None, AXES, None, None),
            P(tables, None),
            P(tables),
            P(tables, None),
            P(tables, None, None),
        ),
        out_specs=(P(tables, None), P(tables)),
        check_vma=False,
    )
```
